256 devices in a mesh: mp: 4 (over z_lo, core), fsdp: 16 (over y, x), dp: 4 (over z_hi).
Axes of the slice: x: 4, y: 4, z: 8 (z_hi: 4, z_lo: 2; z = z_hi * 2 + z_lo), core: 2. Of those that a mesh axis runs over, the one named last changes fastest.
Arguments:
- gen_noise: float32 [4, 4096, 128], P('dp', 'fsdp'), may hold values from -6 to 6
- renoise: float32 [4, 4096, 128], P('dp', 'fsdp'), may hold values from -120 to 120
- gen_step: int32 [4], P('dp'), may hold values from 250 to 999
- renoise_step: int32 [4], P('dp'), may hold values from 20 to 979
- text_pooled: bfloat16 [4, 768], P('dp'), may hold values from -6 to 6
- embed: bfloat16 [3, 64, 3072], replicated, may hold values from -0.75 to 0.75
- mod_weight: bfloat16 [3, 1024, 6144], P(None, None, 'fsdp'), may hold values from -0.1875 to 0.1875
- proj_weight: bfloat16 [3, 3072, 3072], P(None, 'fsdp', 'mp'), may hold values from -0.109375 to 0.109375
- unembed: bfloat16 [3, 64, 3072], P(None, None, 'mp'), may hold values from -0.109375 to 0.109375
Outputs:
- gen_grad: float32 [3072, 3072], P('fsdp', 'mp')
- score_gap: float32 [4, 4096, 128], P('dp', 'fsdp')
The draws below stay inside these ranges and needn't reach their ends.
All inputs are finite; a program needn't handle non-finite values. Where the reference program divides by a largest or mean magnitude, that divisor is 1e-20 or more.
Results may differ from the reference program's by a relative error of at most 0.03.
Values may be sent and summed in bfloat16 or wider, within the bound.
A program may use at most 128 MiB of HBM per device.

```python
import math
import jax
import jax.numpy as jnp
from jax import lax

D = 3072
CH = 64
TXT = 768
TEMB = 256
SEQ = 8192
BATCH = 4
TOKENS = 32768


def draw_renoise(key, part):
    row_key, col_key, base_key = jax.random.split(key, 3)
    pair_rows = SEQ // 2
    position = jnp.arange(pair_rows, dtype=jnp.float32) / pair_rows
    row_factor = jnp.exp(jax.random.uniform(row_key, (BATCH, pair_rows, 1), minval=0.0, maxval=math.log(3.3)))
    col_factor = jnp.exp(jax.random.uniform(col_key, (1, 1, 2 * CH), minval=0.0, maxval=math.log(10.0)))
    rising = jnp.exp(math.log(3.0) * position)[None, :, None]
    base_vals = jnp.clip(jax.random.normal(base_key, (BATCH, pair_rows, 2 * CH)), -6.0, 6.0)
    return (0.2 * base_vals * rising * row_factor * col_factor).astype(jnp.float32)


def set_ends(values, rng, low, top_value):
    dims = values.shape
    place = [jax.random.randint(jax.random.fold_in(rng, axis), (), 0, dims[axis]) for axis in range(len(dims))]
    values = values.at[tuple(place)].set(low)
    longest = dims.index(max(dims))
    place[longest] = (place[longest] + 1) % dims[longest]
    return values.at[tuple(place)].set(top_value)


def level_of(stream_key, extent, cuts, smallest, largest):
    level, own = 1.0, jax.random.fold_in(stream_key, 6)
    for axis_at, shards_of in cuts:
        steps = jnp.exp(jax.random.uniform(jax.random.fold_in(own, axis_at), (shards_of,), jnp.float32, smallest / len(cuts), largest / len(cuts)))
        level = level * jnp.repeat(steps, extent[axis_at] // shards_of).reshape([-1 if axis == axis_at else 1 for axis in range(len(extent))])
    return level


def gaussian(stream_key, dims, width, reach, cuts=(), held_as=jnp.bfloat16):
    loudness = level_of(stream_key, dims, cuts, -0.22, 0.18) if cuts else 1.0
    drawn = jax.random.normal(stream_key, dims, jnp.float32) * width * loudness
    return jnp.minimum(jnp.maximum(drawn, -reach), reach).astype(held_as)


def setup_inputs(seed: int = 0) -> dict:
    seeds = jax.random.split(jax.random.key(seed), 10)
    gen_noise = gaussian(seeds[0], (BATCH, SEQ // 2, 2 * CH), 1.0, 6.0, ((0, 4), (1, 16)), jnp.float32)
    renoise = draw_renoise(jax.random.fold_in(seeds[9], 71), 0)
    gen_step = set_ends(jax.random.randint(seeds[2], (BATCH,), 250, 1000), jax.random.fold_in(seeds[2], 1), 250, 999).astype(jnp.int32)
    renoise_step = set_ends(jax.random.randint(seeds[3], (BATCH,), 20, 980), jax.random.fold_in(seeds[3], 1), 20, 979).astype(jnp.int32)
    text_pooled = gaussian(seeds[4], (BATCH, TXT), 1.0, 6.0, ((0, 4),))
    embed = gaussian(seeds[5], (3, CH, D), CH ** -0.5, 0.75)
    mod_weight = gaussian(seeds[6], (3, TEMB + TXT, 2 * D), (TEMB + TXT) ** -0.5, 0.1875, ((2, 16),))
    proj_weight = gaussian(seeds[7], (3, D, D), D ** -0.5, 0.109375, ((1, 16), (2, 4)))
    unembed = gaussian(seeds[8], (3, CH, D), D ** -0.5, 0.109375, ((2, 4),))
    return {"gen_noise": gen_noise, "renoise": renoise, "gen_step": gen_step, "renoise_step": renoise_step, "text_pooled": text_pooled, "embed": embed, "mod_weight": mod_weight, "proj_weight": proj_weight, "unembed": unembed}


GUIDANCE = 3.5
EPS_NORM = 1e-06
EPS_GAP = 1e-05

def sinusoid(timesteps):
    half_size = TEMB // 2
    frequency = jnp.exp(-math.log(10000.0) * jnp.arange(half_size, dtype=jnp.float32) / half_size)
    angles = timesteps.astype(jnp.float32)[:, None] * frequency[None, :]
    return jnp.concatenate([jnp.cos(angles), jnp.sin(angles)], axis=1)

def condition(timesteps, pooled):
    joined = jnp.concatenate([sinusoid(timesteps), pooled.astype(jnp.float32)], axis=1)
    return jax.nn.silu(joined).astype(jnp.bfloat16)

def normalize(values):
    average = lax.optimization_barrier(jnp.mean(values, axis=1, keepdims=True))
    centred = values - average
    variance = lax.optimization_barrier(jnp.mean(centred * centred, axis=1, keepdims=True))
    return centred * lax.rsqrt(variance + EPS_NORM)

def modulate(normed, modulation):
    return (normed * (1.0 + modulation[D:]) + modulation[:D]).astype(jnp.bfloat16)

def finish(embedded, hidden, weight, out_weight):
    summed = embedded + jnp.dot(hidden, weight, preferred_element_type=jnp.float32)
    return jnp.dot(summed.astype(jnp.bfloat16), out_weight.T, preferred_element_type=jnp.float32)

def reference(gen_noise, renoise, gen_step, renoise_step, text_pooled, embed, mod_weight, proj_weight, unembed):
    blank_text = jnp.zeros_like(text_pooled)
    noisy_vec = condition(renoise_step, text_pooled)
    gen_mod = jnp.dot(condition(gen_step, text_pooled), mod_weight[0], preferred_element_type=jnp.float32)
    cond_mod = jnp.dot(noisy_vec, mod_weight[1], preferred_element_type=jnp.float32)
    blank_mod = jnp.dot(condition(renoise_step, blank_text), mod_weight[1], preferred_element_type=jnp.float32)
    fake_mod = jnp.dot(noisy_vec, mod_weight[2], preferred_element_type=jnp.float32)
    levels = renoise_step.astype(jnp.float32) / 1000.0

    def one_sample(grad_sum, sample_items):
        noise_in, noise_out, gen_row, cond_row, blank_row, fake_row, noise_level = sample_items
        latent = noise_in.reshape(SEQ, CH)
        embedded = jnp.dot(latent.astype(jnp.bfloat16), embed[0], preferred_element_type=jnp.float32)
        gen_hidden = modulate(normalize(embedded), gen_row)
        clean_lat = finish(embedded, gen_hidden, proj_weight[0], unembed[0])
        noisy_lat = (1.0 - noise_level) * clean_lat + noise_level * noise_out.reshape(SEQ, CH)
        noisy_bf = noisy_lat.astype(jnp.bfloat16)
        teacher_in = jnp.dot(noisy_bf, embed[1], preferred_element_type=jnp.float32)
        teacher_norm = normalize(teacher_in)
        cond_out = finish(teacher_in, modulate(teacher_norm, cond_row), proj_weight[1], unembed[1])
        blank_out = finish(teacher_in, modulate(teacher_norm, blank_row), proj_weight[1], unembed[1])
        fake_in = jnp.dot(noisy_bf, embed[2], preferred_element_type=jnp.float32)
        fake_out = finish(fake_in, modulate(normalize(fake_in), fake_row), proj_weight[2], unembed[2])
        real_pred = noisy_lat - noise_level * (blank_out + GUIDANCE * (cond_out - blank_out))
        fake_pred = noisy_lat - noise_level * fake_out
        gap_scale = jnp.mean(jnp.abs(clean_lat - real_pred)) + EPS_GAP
        score_rows = (fake_pred - real_pred) / gap_scale
        cotangent = (score_rows / math.sqrt(TOKENS)).astype(jnp.bfloat16)
        upstream = jnp.dot(cotangent, unembed[0], preferred_element_type=jnp.float32).astype(jnp.bfloat16)
        grad_sum = grad_sum + lax.dot_general(gen_hidden, upstream, (((0,), (0,)), ((), ())), preferred_element_type=jnp.float32)
        return (grad_sum, score_rows.reshape(SEQ // 2, 2 * CH))
    grad_start = jnp.zeros((D, D), jnp.float32)
    gen_grad, score_gap = lax.scan(one_sample, grad_start, (gen_noise, renoise, gen_mod, cond_mod, blank_mod, fake_mod, levels))
    return (gen_grad, score_gap)
```

```python
import math

import jax
import jax.numpy as jnp
from jax import lax
from jax.sharding import PartitionSpec as P

D = 3072
CH = 64
TEMB = 256


GUIDANCE = 3.5
EPS_NORM = 1e-06
EPS_GAP = 1e-05
HIGH = lax.Precision.HIGHEST


def sinusoid(timesteps):
    half_size = TEMB // 2
    frequency = jnp.exp(-math.log(10000.0) * jnp.arange(half_size, dtype=jnp.float32) / half_size)
    angles = timesteps.astype(jnp.float32)[:, None] * frequency[None, :]
    return jnp.concatenate([jnp.cos(angles), jnp.sin(angles)], axis=1)


def condition(timesteps, pooled):
    joined = jnp.concatenate([sinusoid(timesteps), pooled.astype(jnp.float32)], axis=1)
    return jax.nn.silu(joined).astype(jnp.bfloat16)


def mm(left, right):
    return jnp.dot(left, right, precision=HIGH, preferred_element_type=jnp.float32)


def doubled(block):
    zero = jnp.zeros_like(block)
    return jnp.concatenate(
        [jnp.concatenate([block, zero], axis=1), jnp.concatenate([zero, block], axis=1)], axis=0
    )


def body(
    gen_noise, renoise, gen_step, renoise_step, text_pooled, embed, mod_weight, proj_weight, unembed
):
    rows = proj_weight.shape[1]
    quarter = proj_weight.shape[2]
    fsdp_size = lax.axis_size("fsdp")
    row_start = lax.axis_index("fsdp") * rows
    col_start = lax.axis_index("mp") * quarter
    noisy_vec = condition(renoise_step, text_pooled)
    blank_vec = condition(renoise_step, jnp.zeros_like(text_pooled))
    gen_vec = condition(gen_step, text_pooled)
    teacher = jnp.dot(
        jnp.concatenate([noisy_vec, blank_vec], axis=0),
        mod_weight[1],
        preferred_element_type=jnp.float32,
    )
    local_mod = jnp.concatenate(
        [
            jnp.dot(gen_vec, mod_weight[0], preferred_element_type=jnp.float32),
            teacher[1:] + GUIDANCE * (teacher[:1] - teacher[1:]),
            jnp.dot(noisy_vec, mod_weight[2], preferred_element_type=jnp.float32),
        ],
        axis=0,
    )
    modulation = lax.all_gather(local_mod, "fsdp", axis=1, tiled=True)
    shift = lax.dynamic_slice_in_dim(modulation, row_start, rows, 1)
    gain = 1.0 + lax.dynamic_slice_in_dim(modulation, D + row_start, rows, 1)
    wide = embed.astype(jnp.float32)
    centred = wide - jnp.mean(wide, axis=2, keepdims=True)
    spread = jnp.einsum("mcd,med->mce", centred, centred, precision=HIGH) / D
    mine = lax.dynamic_slice_in_dim(centred, row_start, rows, 2)
    folded = jnp.einsum(
        "mrk,mok->mro", proj_weight, unembed, preferred_element_type=jnp.float32
    )
    maps = jnp.einsum("mcr,mro->mco", mine * gain[:, None, :], folded, precision=HIGH)
    offsets = jnp.einsum("mr,mro->mo", shift, folded, precision=HIGH)
    own_cols = lax.dynamic_slice_in_dim(embed, col_start, quarter, 2)
    direct = (
        jnp.einsum("mck,mok->mco", own_cols, unembed, preferred_element_type=jnp.float32)
        / fsdp_size
    )
    total = lax.psum(
        jnp.concatenate([maps, direct, offsets[:, None, :]], axis=1), ("fsdp", "mp")
    )
    maps, direct, offsets = total[:, :CH], total[:, CH : 2 * CH], total[:, 2 * CH :]

    halves = doubled(jnp.ones((CH, CH), jnp.float32))

    def inverse_std(values, which):
        energy = mm(values, doubled(spread[which])) * values
        return lax.rsqrt(jnp.maximum(mm(energy, halves), 0.0) + EPS_NORM)

    def predict(values, scale, which):
        offset = jnp.concatenate([offsets[which], offsets[which]], axis=1)
        return (
            mm(values, doubled(direct[which]))
            + scale * mm(values, doubled(maps[which]))
            + offset
        )

    latent = gen_noise[0].astype(jnp.bfloat16).astype(jnp.float32)
    gen_scale = inverse_std(latent, 0)
    clean_lat = predict(latent, gen_scale, 0)
    noise_level = renoise_step[0].astype(jnp.float32) / 1000.0
    noisy_lat = (1.0 - noise_level) * clean_lat + noise_level * renoise[0]
    noisy = noisy_lat.astype(jnp.bfloat16).astype(jnp.float32)
    real_out = predict(noisy, inverse_std(noisy, 1), 1)
    fake_out = predict(noisy, inverse_std(noisy, 2), 2)
    real_pred = noisy_lat - noise_level * real_out
    raw_gap = noise_level * (real_out - fake_out)
    moment = lax.dot_general(
        (gen_scale * latent).astype(jnp.bfloat16),
        raw_gap.astype(jnp.bfloat16),
        (((0,), (0,)), ((), ())),
        preferred_element_type=jnp.float32,
    )
    moment = moment[:CH, :CH] + moment[CH:, CH:]
    sums = jnp.sum(raw_gap, axis=0)
    sums = sums[:CH] + sums[CH:]
    distance = jnp.full((1, CH), jnp.sum(jnp.abs(clean_lat - real_pred)))
    reduced = lax.psum(jnp.concatenate([moment, sums[None], distance], axis=0), "fsdp")
    seq_len = 2 * gen_noise.shape[1] * fsdp_size
    gap_scale = reduced[CH + 1, 0] / (seq_len * CH) + EPS_GAP
    score_gap = raw_gap / gap_scale
    moment = reduced[: CH + 1] / (gap_scale * math.sqrt(seq_len * lax.axis_size("dp")))
    left = jnp.concatenate([mine[0] * gain[0][None], shift[:1]], axis=0)
    term = lax.dot_general(
        left, moment, (((0,), (0,)), ((), ())), precision=HIGH, preferred_element_type=jnp.float32
    )
    term = lax.psum(term, "dp")
    gen_grad = mm(term, unembed[0].astype(jnp.float32))
    return (gen_grad, score_gap[None])


def solution(mesh):
    return jax.shard_map(
        body,
        mesh=mesh,
        in_specs=(
            P("dp", "fsdp", None),
            P("dp", "fsdp", None),
            P("dp"),
            P("dp"),
            P("dp", None),
            P(),
            P(None, None, "fsdp"),
            P(None, "fsdp", "mp"),
            P(None, None, "mp"),
        ),
        out_specs=(P("fsdp", "mp"), P("dp", "fsdp", None)),
        check_vma=False,
    )
```

```python
import functools
import math

import jax
import jax.numpy as jnp
from jax import lax
from jax.experimental import pallas as pl
from jax.experimental.pallas import tpu as pltpu
from jax.sharding import PartitionSpec as P

D = 3072
CH = 64
TEMB = 256
TXT = 768

GUIDANCE = 3.5
EPS_NORM = 1e-06
EPS_GAP = 1e-05
HIGH = lax.Precision.HIGHEST
MESH = pl.DeviceIdType.MESH
F32 = jnp.float32
BF16 = jnp.bfloat16

MP = 4
DP = 4
NX = 4
NY = 4
SEQ = 8192
TOKENS = 32768
WIN = 384
ROWS = 192
HALF = 96
QUARTER = 768

S_MOD = 0
S_FOLD = 2
S_DIRECT = 5
S_X = 8
S_Y = 11
S_MAPS = 14
S_GEN = 17
S_SUM = 20
S_COL = 35
N_SEM = 50


def split3(values):
    high = values.astype(BF16)
    rest = values - high.astype(F32)
    mid = rest.astype(BF16)
    low = (rest - mid.astype(F32)).astype(BF16)
    return high, mid, low


def split2(values):
    high = values.astype(BF16)
    return high, (values - high.astype(F32)).astype(BF16)


def dot(left, right):
    return jnp.dot(left, right, preferred_element_type=F32)


def dot_nt(left, right):
    return lax.dot_general(left, right, (((1,), (1,)), ((), ())), preferred_element_type=F32)


def pack_pair(block):
    half = block.shape[0] // 2
    return jnp.concatenate([block[:half, :CH], block[half:, :CH]], axis=1)


def lanes(shape):
    return lax.broadcasted_iota(jnp.int32, shape, len(shape) - 1)


def sublanes(shape):
    return lax.broadcasted_iota(jnp.int32, shape, len(shape) - 2)


def doubled(packed):
    left = lanes(packed.shape) < CH
    turned = pltpu.roll(packed, CH, 1)
    zero = jnp.zeros_like(packed)
    return jnp.concatenate(
        [
            jnp.where(left, packed, zero),
            jnp.where(left, turned, zero),
            jnp.where(left, zero, turned),
            jnp.where(left, zero, packed),
        ],
        axis=0,
    )


def kernel(
    gen_noise, renoise, gen_step, renoise_step, text, embed, mod_weight, proj, unembed,
    grad_out, score_out,
    modw_v, proj_v, emb_v, une_v, noise_v, renoise_v, text_v,
    mod_send, mod_recv, fold_send, fold_recv, direct_v,
    x_send, x_recv, y_send, y_recv, maps_v, gen_v,
    mean_v, cov_v, scaled_v, left_v, sum_send, sum_recv, col_v,
    score_v, grad_v,
    load_sem, out_sem, send_sem, recv_sem,
):
    m = lax.axis_index("mp")
    f = lax.axis_index("fsdp")
    d = lax.axis_index("dp")
    y, x = lax.div(f, NX), lax.rem(f, NX)
    pair, side = lax.div(f, 2), lax.rem(f, 2)

    def load(src, dst, slot):
        copy = pltpu.make_async_copy(src, dst, load_sem.at[slot])
        copy.start()
        return copy

    ld_text = load(text, text_v, 0)
    ld_mod = [load(mod_weight.at[k], modw_v.at[k], 1 + k) for k in range(3)]
    ld_une = load(unembed, une_v, 4)
    ld_proj = load(proj, proj_v, 5)
    ld_emb = load(embed, emb_v, 6)
    ld_noise = load(gen_noise.at[0], noise_v, 7)
    ld_renoise = load(renoise.at[0], renoise_v, 8)

    def plane(dy, dx):
        return {"fsdp": lax.rem(y + dy, NY) * NX + lax.rem(x + dx, NX)}

    def column(dd, dm):
        return {"dp": lax.rem(d + dd, DP), "mp": lax.rem(m + dm, MP)}

    plane_steps = [(a, b) for a in range(NY) for b in range(NX) if a or b]
    column_steps = [(a, b) for a in range(DP) for b in range(MP) if a or b]

    barrier = pltpu.get_barrier_semaphore()
    for step in plane_steps:
        pl.semaphore_signal(barrier, inc=1, device_id=plane(*step), device_id_type=MESH)
    for step in column_steps:
        pl.semaphore_signal(barrier, inc=1, device_id=column(*step), device_id_type=MESH)

    def remote(src, dst, slot, device, recv_slot=None):
        return pltpu.make_async_remote_copy(
            src_ref=src,
            dst_ref=dst,
            send_sem=send_sem.at[slot],
            recv_sem=recv_sem.at[slot if recv_slot is None else recv_slot],
            device_id=device,
            device_id_type=MESH,
        )

    t_gen = gen_step[0].astype(F32)
    t_new = renoise_step[0].astype(F32)
    level = t_new / 1000.0
    lane = lanes((8, 128)).astype(F32)
    row8 = sublanes((8, 128))
    frequency = jnp.exp(-math.log(10000.0) * lane / 128)
    angles = jnp.where(row8 == 0, t_gen, t_new) * frequency
    waves = jnp.concatenate([jnp.cos(angles), jnp.sin(angles)], axis=1)
    ld_text.wait()
    words = jnp.broadcast_to(text_v[...].astype(F32), (8, TXT))
    words = jnp.where(sublanes((8, TXT)) < 2, words, 0.0)
    joined = jnp.concatenate([waves, words], axis=1)
    joined = joined / (1.0 + jnp.exp(-joined))
    vectors = jnp.concatenate([joined, jnp.zeros_like(joined)], axis=0).astype(BF16)

    ld_mod[0].wait()
    out0 = dot(vectors, modw_v[0])
    ld_mod[1].wait()
    out1 = dot(vectors, modw_v[1])
    ld_mod[2].wait()
    out2 = dot(vectors, modw_v[2])
    guided = out1[2:3] + GUIDANCE * (out1[1:2] - out1[2:3])
    rows = sublanes((8, WIN))
    mod_send[...] = jnp.where(
        rows == 0, out0[0:1], jnp.where(rows == 1, guided, jnp.where(rows == 2, out2[1:2], 0.0))
    )

    pl.semaphore_wait(barrier, len(plane_steps) + len(column_steps))

    kind = lax.div(f, 8)
    first = 2 * lax.rem(f, 8)

    def mod_copy(k):
        return remote(
            mod_send, mod_recv.at[kind], S_MOD + k, {"fsdp": first + k}, recv_slot=S_MOD + kind
        )

    for k in range(2):
        @pl.when(first + k != f)
        def _():
            mod_copy(k).start()

    @pl.when(f == 0)
    def _():
        mod_recv[0] = mod_send[...]

    @pl.when(f == NX * NY - 1)
    def _():
        mod_recv[1] = mod_send[...]

    ld_une.wait()
    ld_proj.wait()
    for k in range(3):
        fold_send[k] = pack_pair(dot_nt(proj_v[k], une_v[k]))
    ld_emb.wait()
    for k in range(3):
        own = emb_v[k, :, pl.ds(pl.multiple_of(m * QUARTER, 128), QUARTER)]
        fold_send[3, 32 * k : 32 * k + 32, :] = pack_pair(dot_nt(own, une_v[k]))
    fold_copies = []
    for r in range(1, MP):
        target = lax.rem(m + r, MP)
        copy = remote(fold_send.at[target], fold_recv.at[r - 1], S_FOLD + r - 1, {"mp": target})
        copy.start()
        fold_copies.append(copy)

    for k in range(3):
        mean_v[k] = jnp.broadcast_to(
            jnp.mean(emb_v[k].astype(F32), axis=1, keepdims=True), (CH, 128)
        )

    def covariance(k):
        centred = emb_v[k].astype(F32) - mean_v[k][:, :1]
        parts = jnp.concatenate(split3(centred), axis=0)
        gram = dot_nt(parts, parts)
        gram = gram[:CH] + gram[CH : 2 * CH] + gram[2 * CH :]
        gram = (gram[:, :CH] + gram[:, CH : 2 * CH] + gram[:, 2 * CH :]) * (1.0 / D)
        cov_v[k] = jnp.concatenate(split3(doubled(pack_pair(gram))), axis=0)

    covariance(0)

    for copy in fold_copies:
        copy.wait_recv()
    folded = fold_send[m] + fold_recv[0] + fold_recv[1] + fold_recv[2]

    def direct_copy(r):
        return remote(direct_v, direct_v, S_DIRECT + r, {"mp": r}, recv_slot=S_DIRECT)

    @pl.when(m == MP - 1)
    def _():
        direct_v[...] = folded
        for r in range(MP - 1):
            direct_copy(r).start()

    @pl.when(f != 0)
    def _():
        remote(mod_send, mod_recv.at[0], S_MOD, {"fsdp": first}).wait_recv()

    @pl.when(f != NX * NY - 1)
    def _():
        remote(mod_send, mod_recv.at[1], S_MOD + 1, {"fsdp": first}).wait_recv()

    gen_v[d] = jnp.where(
        rows == 0, mod_recv[0, 0:1, :], jnp.where(rows == 1, mod_recv[1, 0:1, :], 0.0)
    )
    gen_copies = []
    for r in range(1, DP):
        copy = remote(gen_v.at[d], gen_v.at[d], S_GEN + r - 1, {"dp": lax.rem(d + r, DP)})
        copy.start()
        gen_copies.append(copy)

    model = jnp.minimum(m, 2)
    window = pl.ds(pl.multiple_of(pair * WIN, 128), WIN)
    shift = mod_recv[0, pl.ds(m, 1), :]
    gain = 1.0 + mod_recv[1, pl.ds(m, 1), :]
    centred = emb_v[model, :, window].astype(F32) - mean_v[model][:, :1]
    left = jnp.concatenate([centred * gain, jnp.broadcast_to(shift, (8, WIN))], axis=0)
    weight = jnp.concatenate([folded[:, :CH], folded[:, CH:]], axis=0)
    none = jnp.zeros_like(weight)
    weight = jnp.concatenate(
        [jnp.where(side == 0, weight, none), jnp.where(side == 0, none, weight)], axis=0
    )
    result = jnp.dot(left, weight, precision=HIGH, preferred_element_type=F32)
    x_send[0:32, :] = pack_pair(result[:CH])
    x_send[32:40, :] = jnp.concatenate([result[CH:], result[CH:]], axis=1)

    x_copies = []
    for r in range(1, NX):
        copy = remote(x_send, x_recv.at[r - 1], S_X + r - 1, plane(0, r))
        copy.start()
        x_copies.append(copy)
    covariance(1)
    for copy in x_copies:
        copy.wait_recv()
    y_send[...] = x_send[...] + x_recv[0] + x_recv[1] + x_recv[2]
    y_copies = []
    for r in range(1, NY):
        copy = remote(y_send, y_recv.at[r - 1], S_Y + r - 1, plane(r, 0))
        copy.start()
        y_copies.append(copy)
    covariance(2)
    for copy in y_copies:
        copy.wait_recv()
    maps_v[m] = y_send[...] + y_recv[0] + y_recv[1] + y_recv[2]
    map_copies = []
    for r in range(1, MP):
        copy = remote(maps_v.at[m], maps_v.at[m], S_MAPS + r - 1, {"mp": lax.rem(m + r, MP)})
        copy.start()
        map_copies.append(copy)

    ones = jnp.where(
        (lanes((128, 128)) < CH) == (sublanes((128, 128)) < CH), 1.0, 0.0
    ).astype(BF16)
    ones = jnp.concatenate([ones, ones, ones], axis=0)

    def inverse_std(values, k):
        thrice = jnp.concatenate([values, values, values], axis=1)
        energy = dot(thrice, cov_v[k]) * values.astype(F32)
        energy = jnp.concatenate(split3(energy), axis=1)
        return lax.rsqrt(jnp.maximum(dot(energy, ones), 0.0) + EPS_NORM)

    def stacked(packed):
        return jnp.concatenate(split2(doubled(packed)), axis=0)

    ld_noise.wait()
    latent = noise_v[...].astype(BF16)
    gen_scale = inverse_std(latent, 0)
    scaled_v[...] = jnp.transpose(latent.astype(F32) * gen_scale).astype(BF16)
    twice = jnp.concatenate([latent, latent], axis=1)

    @pl.when(m != MP - 1)
    def _():
        remote(direct_v, direct_v, S_DIRECT, {"mp": MP - 1}).wait_recv()

    gen_direct = dot(twice, stacked(direct_v[0:32, :]))
    ld_renoise.wait()

    for copy in map_copies:
        copy.wait_recv()
    clean = (
        gen_direct + gen_scale * dot(twice, stacked(maps_v[0, 0:32, :])) + maps_v[0, 32:33, :]
    )
    noisy = (1.0 - level) * clean + level * renoise_v[...]
    values = noisy.astype(BF16)
    twice = jnp.concatenate([values, values], axis=1)
    weights = jnp.concatenate(
        [
            stacked(direct_v[32:64, :]),
            stacked(maps_v[1, 0:32, :]),
            stacked(direct_v[64:96, :]),
            stacked(maps_v[2, 0:32, :]),
        ],
        axis=1,
    )
    products = dot(twice, weights)
    real = products[:, :128] + inverse_std(values, 1) * products[:, 128:256] + maps_v[1, 32:33, :]
    fake = products[:, 256:384] + inverse_std(values, 2) * products[:, 384:] + maps_v[2, 32:33, :]
    gap = level * (real - fake)
    distance = jnp.abs(clean - noisy + level * real)

    moment = dot(scaled_v[...], gap.astype(BF16))
    moment = moment[:CH] + pltpu.roll(moment[CH:], CH, 1)
    left32 = lanes((32, 128)) < CH
    moment = jnp.where(left32, moment[:32], pltpu.roll(moment[32:], CH, 1))
    piece = moment[0:8]
    for k in range(1, MP):
        piece = jnp.where(m == k, moment[8 * k : 8 * k + 8], piece)
    total = jnp.sum(gap, axis=0, keepdims=True)
    total = total + pltpu.roll(total, CH, 1)
    spread = jnp.sum(distance, axis=0, keepdims=True)
    sum_send[0:8, :] = piece
    sum_send[8:16, :] = jnp.where(row8 == 0, total, jnp.where(row8 == 1, spread, 0.0))
    sum_copies = []
    for k, step in enumerate(plane_steps):
        copy = remote(sum_send, sum_recv.at[k], S_SUM + k, plane(*step))
        copy.start()
        sum_copies.append(copy)

    for copy in gen_copies:
        copy.wait_recv()
    centred = emb_v[0, :, window].astype(F32) - mean_v[0][:, :1]
    pieces = [centred[:32] * (1.0 + gen_v[s, 1:2, :]) for s in range(DP)]
    pieces += [centred[32:] * (1.0 + gen_v[s, 1:2, :]) for s in range(DP)]
    pieces += [jnp.where(rows == 0, gen_v[s], 0.0) for s in range(DP)]
    pieces += [jnp.zeros((96, WIN), F32)]
    left_v[...] = jnp.transpose(jnp.concatenate(pieces, axis=0)).astype(BF16)

    for copy in sum_copies:
        copy.wait_recv()
    sums = sum_send[...]
    for k in range(len(plane_steps)):
        sums = sums + sum_recv[k]
    gap_scale = jnp.sum(sums[9:10, :], axis=1, keepdims=True) / (SEQ * CH) + EPS_GAP
    slot = d * MP + m
    col_v[slot] = (sums / (gap_scale * math.sqrt(TOKENS))).astype(BF16)
    col_copies = []
    for k, step in enumerate(column_steps):
        copy = remote(col_v.at[slot], col_v.at[slot], S_COL + k, column(*step))
        copy.start()
        col_copies.append(copy)
    score_v[...] = gap / gap_scale
    score_copy = pltpu.make_async_copy(score_v, score_out.at[0], out_sem.at[0])
    score_copy.start()

    for copy in col_copies:
        copy.wait_recv()
    table = [col_v[k].astype(F32) for k in range(DP * MP)]
    block = jnp.concatenate([entry[:8] for entry in table], axis=0)
    right = jnp.concatenate(
        [block, pltpu.roll(block, CH, 1)]
        + [table[MP * s][8:] for s in range(DP)]
        + [jnp.zeros((96, 128), F32)],
        axis=0,
    ).astype(BF16)
    own_rows = left_v[pl.ds(pl.multiple_of(side * ROWS, 64), ROWS), :]
    term = dot(own_rows, right)[:, :CH].astype(BF16)
    grad_v[...] = dot(term, une_v[0])
    grad_copy = pltpu.make_async_copy(grad_v, grad_out, out_sem.at[1])
    grad_copy.start()

    for k in range(2):
        @pl.when(first + k != f)
        def _():
            mod_copy(k).wait_send()

    @pl.when(m == MP - 1)
    def _():
        for r in range(MP - 1):
            direct_copy(r).wait_send()

    for copy in (
        fold_copies + x_copies + y_copies + map_copies + gen_copies + sum_copies + col_copies
    ):
        copy.wait_send()
    score_copy.wait()
    grad_copy.wait()


def body(
    gen_noise, renoise, gen_step, renoise_step, text_pooled, embed, mod_weight, proj_weight, unembed
):
    hbm = pl.BlockSpec(memory_space=pl.ANY)
    smem = pl.BlockSpec(memory_space=pltpu.SMEM)
    vmem = pltpu.VMEM
    return pl.pallas_call(
        kernel,
        out_shape=(
            jax.ShapeDtypeStruct((ROWS, QUARTER), F32),
            jax.ShapeDtypeStruct(gen_noise.shape, F32),
        ),
        in_specs=[hbm, hbm, smem, smem, hbm, hbm, hbm, hbm, hbm],
        out_specs=(hbm, hbm),
        scratch_shapes=[
            vmem((3, TEMB + TXT, WIN), BF16),
            vmem((3, ROWS, QUARTER), BF16),
            vmem((3, CH, D), BF16),
            vmem((3, CH, QUARTER), BF16),
            vmem((256, 128), F32),
            vmem((256, 128), F32),
            vmem((1, TXT), BF16),
            vmem((8, WIN), F32),
            vmem((2, 8, WIN), F32),
            vmem((4, HALF, 128), F32),
            vmem((3, HALF, 128), F32),
            vmem((HALF, 128), F32),
            vmem((40, 128), F32),
            vmem((3, 40, 128), F32),
            vmem((40, 128), F32),
            vmem((3, 40, 128), F32),
            vmem((4, 40, 128), F32),
            vmem((DP, 8, WIN), F32),
            vmem((3, CH, 128), F32),
            vmem((3, 384, 128), BF16),
            vmem((128, 256), BF16),
            vmem((WIN, 384), BF16),
            vmem((16, 128), F32),
            vmem((15, 16, 128), F32),
            vmem((16, 16, 128), BF16),
            vmem((256, 128), F32),
            vmem((ROWS, QUARTER), F32),
            pltpu.SemaphoreType.DMA((9,)),
            pltpu.SemaphoreType.DMA((2,)),
            pltpu.SemaphoreType.DMA((N_SEM,)),
            pltpu.SemaphoreType.DMA((N_SEM,)),
        ],
        compiler_params=pltpu.CompilerParams(collective_id=0, has_side_effects=True),
        name="distill",
    )(
        gen_noise, renoise, gen_step, renoise_step, text_pooled, embed, mod_weight, proj_weight,
        unembed,
    )


def solution(mesh):
    return jax.shard_map(
        body,
        mesh=mesh,
        in_specs=(
            P("dp", "fsdp", None),
            P("dp", "fsdp", None),
            P("dp"),
            P("dp"),
            P("dp", None),
            P(),
            P(None, None, "fsdp"),
            P(None, "fsdp", "mp"),
            P(None, None, "mp"),
        ),
        out_specs=(P("fsdp", "mp"), P("dp", "fsdp", None)),
        check_vma=False,
    )
```

```python
import functools
import math

import jax
import jax.numpy as jnp
from jax import lax
from jax.experimental import pallas as pl
from jax.experimental.pallas import tpu as pltpu
from jax.sharding import PartitionSpec as P

D = 3072
CH = 64
TEMB = 256
TXT = 768

GUIDANCE = 3.5
EPS_NORM = 1e-06
EPS_GAP = 1e-05
HIGH = lax.Precision.HIGHEST
MESH = pl.DeviceIdType.MESH
F32 = jnp.float32
BF16 = jnp.bfloat16

MP = 4
DP = 4
NX = 4
NY = 4
SEQ = 8192
TOKENS = 32768
WIN = 384
ROWS = 192
HALF = 96
QUARTER = 768

S_MOD = 0
S_FOLD = 2
S_DIRECT = 5
S_X = 8
S_Y = 11
S_MAPS = 14
S_GEN = 17
S_SUM = 20
S_COL = 35
N_SEM = 50


def split3(values):
    high = values.astype(BF16)
    rest = values - high.astype(F32)
    mid = rest.astype(BF16)
    low = (rest - mid.astype(F32)).astype(BF16)
    return high, mid, low


def split2(values):
    high = values.astype(BF16)
    return high, (values - high.astype(F32)).astype(BF16)


def dot(left, right):
    return jnp.dot(left, right, preferred_element_type=F32)


def dot_nt(left, right):
    return lax.dot_general(left, right, (((1,), (1,)), ((), ())), preferred_element_type=F32)


def pack_pair(block):
    half = block.shape[0] // 2
    return jnp.concatenate([block[:half, :CH], block[half:, :CH]], axis=1)


def rounded_map(packed, shift):
    return jnp.concatenate([packed.astype(BF16), *split2(shift)], axis=0)


def summed_map(own, received):
    total = own[...].astype(F32)
    for k in range(3):
        total = total + received[k].astype(F32)
    return rounded_map(total[:32], total[32:40] + total[40:48])


def lanes(shape):
    return lax.broadcasted_iota(jnp.int32, shape, len(shape) - 1)


def sublanes(shape):
    return lax.broadcasted_iota(jnp.int32, shape, len(shape) - 2)


def doubled(packed):
    left = lanes(packed.shape) < CH
    turned = pltpu.roll(packed, CH, 1)
    zero = jnp.zeros_like(packed)
    return jnp.concatenate(
        [
            jnp.where(left, packed, zero),
            jnp.where(left, turned, zero),
            jnp.where(left, zero, turned),
            jnp.where(left, zero, packed),
        ],
        axis=0,
    )


def kernel(
    gen_noise, renoise, gen_step, renoise_step, text, embed, mod_weight, proj, unembed,
    term_out, score_out,
    modw_v, proj_v, emb_v, une_v, noise_v, renoise_v, text_v,
    mod_send, mod_recv, fold_send, fold_recv, direct_v,
    x_send, x_recv, y_send, y_recv, maps_v, gen_v,
    mean_v, cov_v, scaled_v, left_v, sum_send, sum_recv, col_v,
    score_v, term_v, weight_v, centre_v, direct_w,
    load_sem, out_sem, send_sem, recv_sem,
):
    m = lax.axis_index("mp")
    f = lax.axis_index("fsdp")
    d = lax.axis_index("dp")
    y, x = lax.div(f, NX), lax.rem(f, NX)
    pair, side = lax.div(f, 2), lax.rem(f, 2)

    def load(src, dst, slot):
        copy = pltpu.make_async_copy(src, dst, load_sem.at[slot])
        copy.start()
        return copy

    ld_text = load(text, text_v, 0)
    ld_mod = [load(mod_weight.at[k], modw_v.at[k], 1 + k) for k in range(3)]
    ld_une = load(unembed, une_v, 4)
    ld_proj = load(proj, proj_v, 5)
    ld_emb = load(embed, emb_v, 6)
    ld_noise = load(gen_noise.at[0], noise_v, 7)
    ld_renoise = load(renoise.at[0], renoise_v, 8)

    def plane(dy, dx):
        return {"fsdp": lax.rem(y + dy, NY) * NX + lax.rem(x + dx, NX)}

    def column(dd, dm):
        return {"dp": lax.rem(d + dd, DP), "mp": lax.rem(m + dm, MP)}

    def farthest_first(steps):
        return sorted(steps, key=lambda step: -sum(min(n, 4 - n) for n in step))

    plane_steps = farthest_first([(a, b) for a in range(NY) for b in range(NX) if a or b])
    column_steps = farthest_first([(a, b) for a in range(DP) for b in range(MP) if a or b])

    barrier = pltpu.get_barrier_semaphore()
    for step in plane_steps:
        pl.semaphore_signal(barrier, inc=1, device_id=plane(*step), device_id_type=MESH)
    for step in column_steps:
        pl.semaphore_signal(barrier, inc=1, device_id=column(*step), device_id_type=MESH)

    def remote(src, dst, slot, device, recv_slot=None):
        return pltpu.make_async_remote_copy(
            src_ref=src,
            dst_ref=dst,
            send_sem=send_sem.at[slot],
            recv_sem=recv_sem.at[slot if recv_slot is None else recv_slot],
            device_id=device,
            device_id_type=MESH,
        )

    t_gen = gen_step[0].astype(F32)
    t_new = renoise_step[0].astype(F32)
    level = t_new / 1000.0
    lane = lanes((8, 128)).astype(F32)
    row8 = sublanes((8, 128))
    frequency = jnp.exp(-math.log(10000.0) * lane / 128)
    angles = jnp.where(row8 == 0, t_gen, t_new) * frequency
    waves = jnp.concatenate([jnp.cos(angles), jnp.sin(angles)], axis=1)
    ld_text.wait()
    words = jnp.broadcast_to(text_v[...].astype(F32), (8, TXT))
    words = jnp.where(sublanes((8, TXT)) < 2, words, 0.0)
    joined = jnp.concatenate([waves, words], axis=1)
    joined = joined / (1.0 + jnp.exp(-joined))
    vectors = jnp.concatenate([joined, jnp.zeros_like(joined)], axis=0).astype(BF16)

    ld_mod[0].wait()
    out0 = dot(vectors, modw_v[0])
    ld_mod[1].wait()
    out1 = dot(vectors, modw_v[1])
    ld_mod[2].wait()
    out2 = dot(vectors, modw_v[2])
    guided = out1[2:3] + GUIDANCE * (out1[1:2] - out1[2:3])
    rows = sublanes((8, WIN))
    mod_send[...] = jnp.where(
        rows == 0, out0[0:1], jnp.where(rows == 1, guided, jnp.where(rows == 2, out2[1:2], 0.0))
    )

    pl.semaphore_wait(barrier, len(plane_steps) + len(column_steps))

    kind = lax.div(f, 8)
    first = 2 * lax.rem(f, 8)

    def mod_copy(k):
        return remote(
            mod_send, mod_recv.at[kind], S_MOD + k, {"fsdp": first + k}, recv_slot=S_MOD + kind
        )

    for k in range(2):
        @pl.when(first + k != f)
        def _():
            mod_copy(k).start()

    @pl.when(f == 0)
    def _():
        mod_recv[0] = mod_send[...]

    @pl.when(f == NX * NY - 1)
    def _():
        mod_recv[1] = mod_send[...]

    ld_une.wait()
    ld_proj.wait()
    for k in range(3):
        fold_send[k] = pack_pair(dot_nt(proj_v[k], une_v[k]))
    ld_emb.wait()
    for k in range(3):
        own = emb_v[k, :, pl.ds(pl.multiple_of(m * QUARTER, 128), QUARTER)]
        fold_send[3, 32 * k : 32 * k + 32, :] = pack_pair(dot_nt(own, une_v[k]))
    fold_copies = []
    for r in range(1, MP):
        target = lax.rem(m + r, MP)
        copy = remote(fold_send.at[target], fold_recv.at[r - 1], S_FOLD + r - 1, {"mp": target})
        copy.start()
        fold_copies.append(copy)

    for k in range(3):
        mean_v[k] = jnp.broadcast_to(
            jnp.mean(emb_v[k].astype(F32), axis=1, keepdims=True), (CH, 128)
        )

    def covariance(k):
        centred = emb_v[k].astype(F32) - mean_v[k][:, :1]
        parts = jnp.concatenate(split3(centred), axis=0)
        gram = dot_nt(parts, parts)
        gram = gram[:CH] + gram[CH : 2 * CH] + gram[2 * CH :]
        gram = (gram[:, :CH] + gram[:, CH : 2 * CH] + gram[:, 2 * CH :]) * (1.0 / D)
        cov_v[k] = jnp.concatenate(split3(doubled(pack_pair(gram))), axis=0)

    covariance(0)

    for copy in fold_copies:
        copy.wait_recv()
    folded = fold_send[m] + fold_recv[0] + fold_recv[1] + fold_recv[2]

    def direct_copy(r):
        return remote(direct_v, direct_v, S_DIRECT + r, {"mp": r}, recv_slot=S_DIRECT)

    @pl.when(m == MP - 1)
    def _():
        direct_v[...] = folded
        for r in range(MP - 1):
            direct_copy(r).start()

    model = jnp.minimum(m, 2)
    window = pl.ds(pl.multiple_of(pair * WIN, 128), WIN)
    centre_v[...] = emb_v[model, :, window].astype(F32) - mean_v[model][:, :1]
    weight = jnp.concatenate([folded[:, :CH], folded[:, CH:]], axis=0)
    none = jnp.zeros_like(weight)
    weight = jnp.concatenate(
        [jnp.where(side == 0, weight, none), jnp.where(side == 0, none, weight)], axis=0
    )
    high, low = split2(weight)
    weight_v[...] = jnp.concatenate([high, low, high], axis=0)

    @pl.when(f != 0)
    def _():
        remote(mod_send, mod_recv.at[0], S_MOD, {"fsdp": first}).wait_recv()

    @pl.when(f != NX * NY - 1)
    def _():
        remote(mod_send, mod_recv.at[1], S_MOD + 1, {"fsdp": first}).wait_recv()

    shift = mod_recv[0, pl.ds(m, 1), :]
    gain = 1.0 + mod_recv[1, pl.ds(m, 1), :]
    left = jnp.concatenate([centre_v[...] * gain, jnp.broadcast_to(shift, (8, WIN))], axis=0)
    high, low = split2(left)
    result = dot(jnp.concatenate([high, high, low], axis=1), weight_v[...])
    x_send[...] = rounded_map(
        pack_pair(result[:CH]), jnp.concatenate([result[CH:], result[CH:]], axis=1)
    )

    x_copies = []
    for r in range(1, NX):
        copy = remote(x_send, x_recv.at[r - 1], S_X + r - 1, plane(0, r))
        copy.start()
        x_copies.append(copy)

    gen_v[d] = jnp.where(
        rows == 0, mod_recv[0, 0:1, :], jnp.where(rows == 1, mod_recv[1, 0:1, :], 0.0)
    )
    gen_copies = []
    for r in range(1, DP):
        copy = remote(gen_v.at[d], gen_v.at[d], S_GEN + r - 1, {"dp": lax.rem(d + r, DP)})
        copy.start()
        gen_copies.append(copy)

    covariance(1)
    for copy in x_copies:
        copy.wait_recv()
    y_send[...] = summed_map(x_send, x_recv)
    y_copies = []
    for r in range(1, NY):
        copy = remote(y_send, y_recv.at[r - 1], S_Y + r - 1, plane(r, 0))
        copy.start()
        y_copies.append(copy)
    covariance(2)
    for copy in y_copies:
        copy.wait_recv()
    maps_v[m] = summed_map(y_send, y_recv)
    map_copies = []
    for r in range(1, MP):
        copy = remote(maps_v.at[m], maps_v.at[m], S_MAPS + r - 1, {"mp": lax.rem(m + r, MP)})
        copy.start()
        map_copies.append(copy)

    ones = jnp.where(
        (lanes((128, 128)) < CH) == (sublanes((128, 128)) < CH), 1.0, 0.0
    ).astype(BF16)
    ones = jnp.concatenate([ones, ones, ones], axis=0)

    def inverse_std(values, k):
        thrice = jnp.concatenate([values, values, values], axis=1)
        energy = dot(thrice, cov_v[k]) * values.astype(F32)
        energy = jnp.concatenate(split3(energy), axis=1)
        return lax.rsqrt(jnp.maximum(dot(energy, ones), 0.0) + EPS_NORM)

    def stacked(packed):
        return jnp.concatenate(split2(doubled(packed)), axis=0)

    ld_noise.wait()
    latent = noise_v[...].astype(BF16)
    gen_scale = inverse_std(latent, 0)
    scaled_v[...] = jnp.transpose(latent.astype(F32) * gen_scale).astype(BF16)
    twice = jnp.concatenate([latent, latent], axis=1)

    @pl.when(m != MP - 1)
    def _():
        remote(direct_v, direct_v, S_DIRECT, {"mp": MP - 1}).wait_recv()

    gen_direct = dot(twice, stacked(direct_v[0:32, :]))
    direct_w[:, :128] = stacked(direct_v[32:64, :])
    direct_w[:, 128:] = stacked(direct_v[64:96, :])
    ld_renoise.wait()

    for copy in map_copies:
        copy.wait_recv()

    def map_of(k):
        return doubled(maps_v[k, 0:32, :].astype(F32)).astype(BF16)

    def shift_of(k):
        rows16 = maps_v[k, 32:48, :].astype(F32)
        return rows16[0:1] + rows16[8:9]

    clean = gen_direct + gen_scale * dot(latent, map_of(0)) + shift_of(0)
    noisy = (1.0 - level) * clean + level * renoise_v[...]
    values = noisy.astype(BF16)
    twice = jnp.concatenate([values, values], axis=1)
    direct = dot(twice, direct_w[...])
    mapped = dot(values, jnp.concatenate([map_of(1), map_of(2)], axis=1))
    real = direct[:, :128] + inverse_std(values, 1) * mapped[:, :128] + shift_of(1)
    fake = direct[:, 128:] + inverse_std(values, 2) * mapped[:, 128:] + shift_of(2)
    gap = level * (real - fake)
    distance = jnp.abs(clean - noisy + level * real)

    moment = dot(scaled_v[...], gap.astype(BF16))
    moment = moment[:CH] + pltpu.roll(moment[CH:], CH, 1)
    left32 = lanes((32, 128)) < CH
    moment = jnp.where(left32, moment[:32], pltpu.roll(moment[32:], CH, 1))
    piece = moment[0:8]
    for k in range(1, MP):
        piece = jnp.where(m == k, moment[8 * k : 8 * k + 8], piece)
    total = jnp.sum(gap, axis=0, keepdims=True)
    total = total + pltpu.roll(total, CH, 1)
    spread = jnp.sum(distance, axis=0, keepdims=True)
    tail = []
    for term in split2(total) + split2(spread):
        tail.append(jnp.broadcast_to(term.astype(F32), (8, 128)))
    tail = jnp.where(
        row8 == 0, tail[0], jnp.where(row8 == 1, tail[1], jnp.where(row8 == 2, tail[2], tail[3]))
    )
    tail = jnp.where(row8 < 4, tail, 0.0)
    sum_send[...] = jnp.concatenate([piece, tail], axis=0).astype(BF16)
    sum_copies = []
    for k, step in enumerate(plane_steps):
        copy = remote(sum_send, sum_recv.at[k], S_SUM + k, plane(*step))
        copy.start()
        sum_copies.append(copy)

    for copy in gen_copies:
        copy.wait_recv()
    centred = emb_v[0, :, window].astype(F32) - mean_v[0][:, :1]
    pieces = [centred[:32] * (1.0 + gen_v[s, 1:2, :]) for s in range(DP)]
    pieces += [centred[32:] * (1.0 + gen_v[s, 1:2, :]) for s in range(DP)]
    pieces += [jnp.where(rows == 0, gen_v[s], 0.0) for s in range(DP)]
    pieces += [jnp.zeros((96, WIN), F32)]
    left_v[...] = jnp.transpose(jnp.concatenate(pieces, axis=0)).astype(BF16)

    for copy in sum_copies:
        copy.wait_recv()
    sums = sum_send[...].astype(F32)
    for k in range(len(plane_steps)):
        sums = sums + sum_recv[k].astype(F32)
    spread = sums[10:11, :] + sums[11:12, :]
    gap_scale = jnp.sum(spread, axis=1, keepdims=True) / (SEQ * CH) + EPS_GAP
    total = jnp.where(row8 == 0, sums[8:9, :] + sums[9:10, :], 0.0)
    sums = jnp.concatenate([sums[0:8], total], axis=0)
    slot = d * MP + m
    col_v[slot] = (sums / (gap_scale * math.sqrt(TOKENS))).astype(BF16)
    col_copies = []
    for k, step in enumerate(column_steps):
        copy = remote(col_v.at[slot], col_v.at[slot], S_COL + k, column(*step))
        copy.start()
        col_copies.append(copy)
    score_v[...] = gap / gap_scale
    score_copy = pltpu.make_async_copy(score_v, score_out.at[0], out_sem.at[0])
    score_copy.start()

    for copy in col_copies:
        copy.wait_recv()
    table = [col_v[k].astype(F32) for k in range(DP * MP)]
    block = jnp.concatenate([entry[:8] for entry in table], axis=0)
    right = jnp.concatenate(
        [block, pltpu.roll(block, CH, 1)]
        + [table[MP * s][8:] for s in range(DP)]
        + [jnp.zeros((96, 128), F32)],
        axis=0,
    ).astype(BF16)
    own_rows = left_v[pl.ds(pl.multiple_of(side * ROWS, 64), ROWS), :]
    term_v[...] = dot(own_rows, right).astype(BF16)
    term_copy = pltpu.make_async_copy(term_v, term_out, out_sem.at[1])
    term_copy.start()

    for k in range(2):
        @pl.when(first + k != f)
        def _():
            mod_copy(k).wait_send()

    @pl.when(m == MP - 1)
    def _():
        for r in range(MP - 1):
            direct_copy(r).wait_send()

    for copy in (
        fold_copies + x_copies + y_copies + map_copies + gen_copies + sum_copies + col_copies
    ):
        copy.wait_send()
    score_copy.wait()
    term_copy.wait()


def finish(
    term, unembed, score, grad_out, score_out, term_v, une_v, score_v, grad_v, in_sem, out_sem
):
    loads = [
        pltpu.make_async_copy(src, dst, in_sem.at[k])
        for k, (src, dst) in enumerate(
            [(term, term_v), (unembed.at[0], une_v), (score.at[0], score_v)]
        )
    ]
    for copy in loads:
        copy.start()
    loads[0].wait()
    loads[1].wait()
    stores = []
    for k in range(2):
        rows = slice(HALF * k, HALF * k + HALF)
        grad_v[rows, :] = dot(term_v[rows, :CH], une_v[...])
        copy = pltpu.make_async_copy(grad_v.at[rows], grad_out.at[rows], out_sem.at[k])
        copy.start()
        stores.append(copy)
    loads[2].wait()
    copy = pltpu.make_async_copy(score_v, score_out.at[0], out_sem.at[2])
    copy.start()
    stores.append(copy)
    for copy in stores:
        copy.wait()


def body(
    gen_noise, renoise, gen_step, renoise_step, text_pooled, embed, mod_weight, proj_weight, unembed
):
    hbm = pl.BlockSpec(memory_space=pl.ANY)
    smem = pl.BlockSpec(memory_space=pltpu.SMEM)
    vmem = pltpu.VMEM
    term, score = pl.pallas_call(
        kernel,
        out_shape=(
            jax.ShapeDtypeStruct((ROWS, 128), BF16),
            jax.ShapeDtypeStruct(gen_noise.shape, F32),
        ),
        in_specs=[hbm, hbm, smem, smem, hbm, hbm, hbm, hbm, hbm],
        out_specs=(hbm, hbm),
        scratch_shapes=[
            vmem((3, TEMB + TXT, WIN), BF16),
            vmem((3, ROWS, QUARTER), BF16),
            vmem((3, CH, D), BF16),
            vmem((3, CH, QUARTER), BF16),
            vmem((256, 128), F32),
            vmem((256, 128), F32),
            vmem((1, TXT), BF16),
            vmem((8, WIN), F32),
            vmem((2, 8, WIN), F32),
            vmem((4, HALF, 128), F32),
            vmem((3, HALF, 128), F32),
            vmem((HALF, 128), F32),
            vmem((48, 128), BF16),
            vmem((3, 48, 128), BF16),
            vmem((48, 128), BF16),
            vmem((3, 48, 128), BF16),
            vmem((4, 48, 128), BF16),
            vmem((DP, 8, WIN), F32),
            vmem((3, CH, 128), F32),
            vmem((3, 384, 128), BF16),
            vmem((128, 256), BF16),
            vmem((WIN, 384), BF16),
            vmem((16, 128), BF16),
            vmem((15, 16, 128), BF16),
            vmem((16, 16, 128), BF16),
            vmem((256, 128), F32),
            vmem((ROWS, 128), BF16),
            vmem((3 * WIN, CH), BF16),
            vmem((CH, WIN), F32),
            vmem((256, 256), BF16),
            pltpu.SemaphoreType.DMA((9,)),
            pltpu.SemaphoreType.DMA((2,)),
            pltpu.SemaphoreType.DMA((N_SEM,)),
            pltpu.SemaphoreType.DMA((N_SEM,)),
        ],
        compiler_params=pltpu.CompilerParams(collective_id=0, has_side_effects=True),
        name="distill",
    )(
        gen_noise, renoise, gen_step, renoise_step, text_pooled, embed, mod_weight, proj_weight,
        unembed,
    )
    return pl.pallas_call(
        finish,
        out_shape=(
            jax.ShapeDtypeStruct((ROWS, QUARTER), F32),
            jax.ShapeDtypeStruct(gen_noise.shape, F32),
        ),
        in_specs=[hbm, hbm, hbm],
        out_specs=(hbm, hbm),
        scratch_shapes=[
            vmem((ROWS, 128), BF16),
            vmem((CH, QUARTER), BF16),
            vmem((256, 128), F32),
            vmem((ROWS, QUARTER), F32),
            pltpu.SemaphoreType.DMA((3,)),
            pltpu.SemaphoreType.DMA((3,)),
        ],
        name="finish",
    )(term, unembed, score)


def solution(mesh):
    return jax.shard_map(
        body,
        mesh=mesh,
        in_specs=(
            P("dp", "fsdp", None),
            P("dp", "fsdp", None),
            P("dp"),
            P("dp"),
            P("dp", None),
            P(),
            P(None, None, "fsdp"),
            P(None, "fsdp", "mp"),
            P(None, None, "mp"),
        ),
        out_specs=(P("fsdp", "mp"), P("dp", "fsdp", None)),
        check_vma=False,
    )
```

```python
import functools
import math

import jax
import jax.numpy as jnp
from jax import lax
from jax.experimental import pallas as pl
from jax.experimental.pallas import tpu as pltpu
from jax.sharding import PartitionSpec as P

D = 3072
CH = 64
TEMB = 256
TXT = 768

GUIDANCE = 3.5
EPS_NORM = 1e-06
EPS_GAP = 1e-05
HIGH = lax.Precision.HIGHEST
MESH = pl.DeviceIdType.MESH
F32 = jnp.float32
BF16 = jnp.bfloat16

MP = 4
DP = 4
NX = 4
NY = 4
SEQ = 8192
TOKENS = 32768
WIN = 384
ROWS = 192
HALF = 96
QUARTER = 768

S_MOD = 0
S_FOLD = 2
S_DIRECT = 5
S_X = 8
S_Y = 11
S_MAPS = 14
S_GEN = 17
S_SUM = 20
S_COL = 35
N_SEM = 50


def split3(values):
    high = values.astype(BF16)
    rest = values - high.astype(F32)
    mid = rest.astype(BF16)
    low = (rest - mid.astype(F32)).astype(BF16)
    return high, mid, low


def split2(values):
    high = values.astype(BF16)
    return high, (values - high.astype(F32)).astype(BF16)


def dot(left, right):
    return jnp.dot(left, right, preferred_element_type=F32)


def dot_nt(left, right):
    return lax.dot_general(left, right, (((1,), (1,)), ((), ())), preferred_element_type=F32)


def pack_pair(block):
    half = block.shape[0] // 2
    return jnp.concatenate([block[:half, :CH], block[half:, :CH]], axis=1)


def rounded_map(packed, shift):
    return jnp.concatenate([packed.astype(BF16), *split2(shift)], axis=0)


def summed_map(own, received):
    total = own[...].astype(F32)
    for k in range(3):
        total = total + received[k].astype(F32)
    return rounded_map(total[:32], total[32:40] + total[40:48])


def lanes(shape):
    return lax.broadcasted_iota(jnp.int32, shape, len(shape) - 1)


def sublanes(shape):
    return lax.broadcasted_iota(jnp.int32, shape, len(shape) - 2)


def doubled(packed):
    left = lanes(packed.shape) < CH
    turned = pltpu.roll(packed, CH, 1)
    zero = jnp.zeros_like(packed)
    return jnp.concatenate(
        [
            jnp.where(left, packed, zero),
            jnp.where(left, turned, zero),
            jnp.where(left, zero, turned),
            jnp.where(left, zero, packed),
        ],
        axis=0,
    )


def kernel(
    gen_noise, renoise, gen_step, renoise_step, text, embed, mod_weight, proj, unembed,
    term_out, score_out,
    modw_v, proj_v, emb_v, une_v, noise_v, renoise_v, text_v,
    mod_send, mod_recv, fold_send, fold_recv, direct_v,
    x_send, x_recv, y_send, y_recv, maps_v, gen_v,
    mean_v, cov_v, scaled_v, left_v, sum_send, sum_recv, col_v,
    score_v, term_v, weight_v, centre_v, direct_w,
    load_sem, out_sem, send_sem, recv_sem,
):
    m = lax.axis_index("mp")
    f = lax.axis_index("fsdp")
    d = lax.axis_index("dp")
    y, x = lax.div(f, NX), lax.rem(f, NX)
    pair, side = lax.div(f, 2), lax.rem(f, 2)

    def load(src, dst, slot):
        copy = pltpu.make_async_copy(src, dst, load_sem.at[slot])
        copy.start()
        return copy

    ld_text = load(text, text_v, 0)
    ld_mod = [load(mod_weight.at[k], modw_v.at[k], 1 + k) for k in range(3)]
    ld_une = load(unembed, une_v, 4)
    ld_proj = load(proj, proj_v, 5)

    def plane(dy, dx):
        return {"fsdp": lax.rem(y + dy, NY) * NX + lax.rem(x + dx, NX)}

    def column(dd, dm):
        return {"dp": lax.rem(d + dd, DP), "mp": lax.rem(m + dm, MP)}

    def farthest_first(steps):
        return sorted(steps, key=lambda step: -sum(min(n, 4 - n) for n in step))

    plane_steps = farthest_first([(a, b) for a in range(NY) for b in range(NX) if a or b])
    column_steps = farthest_first([(a, b) for a in range(DP) for b in range(MP) if a or b])

    barrier = pltpu.get_barrier_semaphore()
    for step in plane_steps:
        pl.semaphore_signal(barrier, inc=1, device_id=plane(*step), device_id_type=MESH)
    for step in column_steps:
        pl.semaphore_signal(barrier, inc=1, device_id=column(*step), device_id_type=MESH)

    def remote(src, dst, slot, device, recv_slot=None):
        return pltpu.make_async_remote_copy(
            src_ref=src,
            dst_ref=dst,
            send_sem=send_sem.at[slot],
            recv_sem=recv_sem.at[slot if recv_slot is None else recv_slot],
            device_id=device,
            device_id_type=MESH,
        )

    t_gen = gen_step[0].astype(F32)
    t_new = renoise_step[0].astype(F32)
    level = t_new / 1000.0
    lane = lanes((8, 128)).astype(F32)
    row8 = sublanes((8, 128))
    frequency = jnp.exp(-math.log(10000.0) * lane / 128)
    angles = jnp.where(row8 == 0, t_gen, t_new) * frequency
    waves = jnp.concatenate([jnp.cos(angles), jnp.sin(angles)], axis=1)
    ld_text.wait()
    words = jnp.broadcast_to(text_v[...].astype(F32), (8, TXT))
    words = jnp.where(sublanes((8, TXT)) < 2, words, 0.0)
    joined = jnp.concatenate([waves, words], axis=1)
    joined = joined / (1.0 + jnp.exp(-joined))
    vectors = jnp.concatenate([joined, jnp.zeros_like(joined)], axis=0).astype(BF16)

    ld_mod[0].wait()
    ld_emb = load(embed, emb_v, 6)
    out0 = dot(vectors, modw_v[0])
    ld_mod[1].wait()
    out1 = dot(vectors, modw_v[1])
    ld_mod[2].wait()
    ld_noise = load(gen_noise.at[0], noise_v, 7)
    ld_renoise = load(renoise.at[0], renoise_v, 8)
    out2 = dot(vectors, modw_v[2])
    guided = out1[2:3] + GUIDANCE * (out1[1:2] - out1[2:3])
    rows = sublanes((8, WIN))
    mod_send[...] = jnp.where(
        rows == 0, out0[0:1], jnp.where(rows == 1, guided, jnp.where(rows == 2, out2[1:2], 0.0))
    )

    pl.semaphore_wait(barrier, len(plane_steps) + len(column_steps))

    kind = lax.div(f, 8)
    first = 2 * lax.rem(f, 8)

    def mod_copy(k):
        return remote(
            mod_send, mod_recv.at[kind], S_MOD + k, {"fsdp": first + k}, recv_slot=S_MOD + kind
        )

    for k in range(2):
        @pl.when(first + k != f)
        def _():
            mod_copy(k).start()

    @pl.when(f == 0)
    def _():
        mod_recv[0] = mod_send[...]

    @pl.when(f == NX * NY - 1)
    def _():
        mod_recv[1] = mod_send[...]

    ld_une.wait()
    ld_proj.wait()
    for k in range(3):
        fold_send[k] = pack_pair(dot_nt(proj_v[k], une_v[k])).astype(BF16)
    ld_emb.wait()
    for k in range(3):
        own = emb_v[k, :, pl.ds(pl.multiple_of(m * QUARTER, 128), QUARTER)]
        fold_send[3, 32 * k : 32 * k + 32, :] = pack_pair(dot_nt(own, une_v[k])).astype(BF16)
    fold_copies = []
    for r in range(1, MP):
        target = lax.rem(m + r, MP)
        copy = remote(fold_send.at[target], fold_recv.at[r - 1], S_FOLD + r - 1, {"mp": target})
        copy.start()
        fold_copies.append(copy)

    for k in range(3):
        mean_v[k] = jnp.broadcast_to(
            jnp.mean(emb_v[k].astype(F32), axis=1, keepdims=True), (CH, 128)
        )

    def covariance(k):
        centred = emb_v[k].astype(F32) - mean_v[k][:, :1]
        parts = jnp.concatenate(split3(centred), axis=0)
        gram = dot_nt(parts, parts)
        gram = gram[:CH] + gram[CH : 2 * CH] + gram[2 * CH :]
        gram = (gram[:, :CH] + gram[:, CH : 2 * CH] + gram[:, 2 * CH :]) * (1.0 / D)
        cov_v[k] = jnp.concatenate(split3(doubled(pack_pair(gram))), axis=0)

    covariance(0)

    for copy in fold_copies:
        copy.wait_recv()
    folded = fold_send[m].astype(F32)
    for r in range(MP - 1):
        folded = folded + fold_recv[r].astype(F32)

    def direct_copy(r):
        return remote(direct_v, direct_v, S_DIRECT + r, {"mp": r}, recv_slot=S_DIRECT)

    @pl.when(m == MP - 1)
    def _():
        direct_v[...] = folded
        for r in range(MP - 1):
            direct_copy(r).start()

    model = jnp.minimum(m, 2)
    window = pl.ds(pl.multiple_of(pair * WIN, 128), WIN)
    centre_v[...] = emb_v[model, :, window].astype(F32) - mean_v[model][:, :1]
    weight = jnp.concatenate([folded[:, :CH], folded[:, CH:]], axis=0)
    none = jnp.zeros_like(weight)
    weight = jnp.concatenate(
        [jnp.where(side == 0, weight, none), jnp.where(side == 0, none, weight)], axis=0
    )
    high, low = split2(weight)
    weight_v[...] = jnp.concatenate([high, low, high], axis=0)

    @pl.when(f != 0)
    def _():
        remote(mod_send, mod_recv.at[0], S_MOD, {"fsdp": first}).wait_recv()

    @pl.when(f != NX * NY - 1)
    def _():
        remote(mod_send, mod_recv.at[1], S_MOD + 1, {"fsdp": first}).wait_recv()

    shift = mod_recv[0, pl.ds(m, 1), :]
    gain = 1.0 + mod_recv[1, pl.ds(m, 1), :]
    left = jnp.concatenate([centre_v[...] * gain, jnp.broadcast_to(shift, (8, WIN))], axis=0)
    high, low = split2(left)
    result = dot(jnp.concatenate([high, high, low], axis=1), weight_v[...])
    x_send[...] = rounded_map(
        pack_pair(result[:CH]), jnp.concatenate([result[CH:], result[CH:]], axis=1)
    )

    x_copies = []
    for r in range(1, NX):
        copy = remote(x_send, x_recv.at[r - 1], S_X + r - 1, plane(0, r))
        copy.start()
        x_copies.append(copy)

    gen_v[d] = jnp.where(
        rows == 0, mod_recv[0, 0:1, :], jnp.where(rows == 1, mod_recv[1, 0:1, :], 0.0)
    )
    gen_copies = []
    for r in range(1, DP):
        copy = remote(gen_v.at[d], gen_v.at[d], S_GEN + r - 1, {"dp": lax.rem(d + r, DP)})
        copy.start()
        gen_copies.append(copy)

    covariance(1)
    for copy in x_copies:
        copy.wait_recv()
    y_send[...] = summed_map(x_send, x_recv)
    y_copies = []
    for r in range(1, NY):
        copy = remote(y_send, y_recv.at[r - 1], S_Y + r - 1, plane(r, 0))
        copy.start()
        y_copies.append(copy)
    covariance(2)
    for copy in y_copies:
        copy.wait_recv()
    maps_v[m] = summed_map(y_send, y_recv)
    map_copies = []
    for r in range(1, MP):
        copy = remote(maps_v.at[m], maps_v.at[m], S_MAPS + r - 1, {"mp": lax.rem(m + r, MP)})
        copy.start()
        map_copies.append(copy)

    ones = jnp.where(
        (lanes((128, 128)) < CH) == (sublanes((128, 128)) < CH), 1.0, 0.0
    ).astype(BF16)
    ones = jnp.concatenate([ones, ones, ones], axis=0)

    def inverse_std(values, k):
        thrice = jnp.concatenate([values, values, values], axis=1)
        energy = dot(thrice, cov_v[k]) * values.astype(F32)
        energy = jnp.concatenate(split3(energy), axis=1)
        return lax.rsqrt(jnp.maximum(dot(energy, ones), 0.0) + EPS_NORM)

    def stacked(packed):
        return jnp.concatenate(split2(doubled(packed)), axis=0)

    ld_noise.wait()
    latent = noise_v[...].astype(BF16)
    gen_scale = inverse_std(latent, 0)
    scaled_v[...] = jnp.transpose(latent.astype(F32) * gen_scale).astype(BF16)
    twice = jnp.concatenate([latent, latent], axis=1)

    @pl.when(m != MP - 1)
    def _():
        remote(direct_v, direct_v, S_DIRECT, {"mp": MP - 1}).wait_recv()

    gen_direct = dot(twice, stacked(direct_v[0:32, :]))
    direct_w[:, :128] = stacked(direct_v[32:64, :])
    direct_w[:, 128:] = stacked(direct_v[64:96, :])
    ld_renoise.wait()

    for copy in map_copies:
        copy.wait_recv()

    def map_of(k):
        return doubled(maps_v[k, 0:32, :].astype(F32)).astype(BF16)

    def shift_of(k):
        rows16 = maps_v[k, 32:48, :].astype(F32)
        return rows16[0:1] + rows16[8:9]

    clean = gen_direct + gen_scale * dot(latent, map_of(0)) + shift_of(0)
    noisy = (1.0 - level) * clean + level * renoise_v[...]
    values = noisy.astype(BF16)
    twice = jnp.concatenate([values, values], axis=1)
    direct = dot(twice, direct_w[...])
    mapped = dot(values, jnp.concatenate([map_of(1), map_of(2)], axis=1))
    real = direct[:, :128] + inverse_std(values, 1) * mapped[:, :128] + shift_of(1)
    fake = direct[:, 128:] + inverse_std(values, 2) * mapped[:, 128:] + shift_of(2)
    gap = level * (real - fake)
    distance = jnp.abs(clean - noisy + level * real)

    moment = dot(scaled_v[...], gap.astype(BF16))
    moment = moment[:CH] + pltpu.roll(moment[CH:], CH, 1)
    left32 = lanes((32, 128)) < CH
    moment = jnp.where(left32, moment[:32], pltpu.roll(moment[32:], CH, 1))
    piece = moment[0:8]
    for k in range(1, MP):
        piece = jnp.where(m == k, moment[8 * k : 8 * k + 8], piece)
    total = jnp.sum(gap, axis=0, keepdims=True)
    total = total + pltpu.roll(total, CH, 1)
    spread = jnp.sum(distance, axis=0, keepdims=True)
    tail = []
    for term in split2(total) + split2(spread):
        tail.append(jnp.broadcast_to(term.astype(F32), (8, 128)))
    tail = jnp.where(
        row8 == 0, tail[0], jnp.where(row8 == 1, tail[1], jnp.where(row8 == 2, tail[2], tail[3]))
    )
    tail = jnp.where(row8 < 4, tail, 0.0)
    sum_send[...] = jnp.concatenate([piece, tail], axis=0).astype(BF16)
    sum_copies = []
    for k, step in enumerate(plane_steps):
        copy = remote(sum_send, sum_recv.at[k], S_SUM + k, plane(*step))
        copy.start()
        sum_copies.append(copy)

    for copy in gen_copies:
        copy.wait_recv()
    centred = emb_v[0, :, window].astype(F32) - mean_v[0][:, :1]
    pieces = [centred[:32] * (1.0 + gen_v[s, 1:2, :]) for s in range(DP)]
    pieces += [centred[32:] * (1.0 + gen_v[s, 1:2, :]) for s in range(DP)]
    pieces += [jnp.where(rows == 0, gen_v[s], 0.0) for s in range(DP)]
    pieces += [jnp.zeros((96, WIN), F32)]
    left_v[...] = jnp.transpose(jnp.concatenate(pieces, axis=0)).astype(BF16)

    for copy in sum_copies:
        copy.wait_recv()
    sums = sum_send[...].astype(F32)
    for k in range(len(plane_steps)):
        sums = sums + sum_recv[k].astype(F32)
    spread = sums[10:11, :] + sums[11:12, :]
    gap_scale = jnp.sum(spread, axis=1, keepdims=True) / (SEQ * CH) + EPS_GAP
    total = jnp.where(row8 == 0, sums[8:9, :] + sums[9:10, :], 0.0)
    sums = jnp.concatenate([sums[0:8], total], axis=0)
    slot = d * MP + m
    col_v[slot] = (sums / (gap_scale * math.sqrt(TOKENS))).astype(BF16)
    col_copies = []
    for k, step in enumerate(column_steps):
        copy = remote(col_v.at[slot], col_v.at[slot], S_COL + k, column(*step))
        copy.start()
        col_copies.append(copy)
    score_v[...] = gap / gap_scale
    score_copy = pltpu.make_async_copy(score_v, score_out.at[0], out_sem.at[0])
    score_copy.start()

    for copy in col_copies:
        copy.wait_recv()
    table = [col_v[k].astype(F32) for k in range(DP * MP)]
    block = jnp.concatenate([entry[:8] for entry in table], axis=0)
    right = jnp.concatenate(
        [block, pltpu.roll(block, CH, 1)]
        + [table[MP * s][8:] for s in range(DP)]
        + [jnp.zeros((96, 128), F32)],
        axis=0,
    ).astype(BF16)
    own_rows = left_v[pl.ds(pl.multiple_of(side * ROWS, 64), ROWS), :]
    term_v[...] = dot(own_rows, right).astype(BF16)
    term_copy = pltpu.make_async_copy(term_v, term_out, out_sem.at[1])
    term_copy.start()

    for k in range(2):
        @pl.when(first + k != f)
        def _():
            mod_copy(k).wait_send()

    @pl.when(m == MP - 1)
    def _():
        for r in range(MP - 1):
            direct_copy(r).wait_send()

    for copy in (
        fold_copies + x_copies + y_copies + map_copies + gen_copies + sum_copies + col_copies
    ):
        copy.wait_send()
    score_copy.wait()
    term_copy.wait()


def finish(
    term, unembed, score, grad_out, score_out, term_v, une_v, score_v, grad_v, in_sem, out_sem
):
    loads = [
        pltpu.make_async_copy(src, dst, in_sem.at[k])
        for k, (src, dst) in enumerate(
            [(term, term_v), (unembed.at[0], une_v), (score.at[0], score_v)]
        )
    ]
    for copy in loads:
        copy.start()
    loads[0].wait()
    loads[1].wait()
    stores = []
    for k in range(2):
        rows = slice(HALF * k, HALF * k + HALF)
        grad_v[rows, :] = dot(term_v[rows, :CH], une_v[...])
        copy = pltpu.make_async_copy(grad_v.at[rows], grad_out.at[rows], out_sem.at[k])
        copy.start()
        stores.append(copy)
    loads[2].wait()
    copy = pltpu.make_async_copy(score_v, score_out.at[0], out_sem.at[2])
    copy.start()
    stores.append(copy)
    for copy in stores:
        copy.wait()


def body(
    gen_noise, renoise, gen_step, renoise_step, text_pooled, embed, mod_weight, proj_weight, unembed
):
    hbm = pl.BlockSpec(memory_space=pl.ANY)
    smem = pl.BlockSpec(memory_space=pltpu.SMEM)
    vmem = pltpu.VMEM
    term, score = pl.pallas_call(
        kernel,
        out_shape=(
            jax.ShapeDtypeStruct((ROWS, 128), BF16),
            jax.ShapeDtypeStruct(gen_noise.shape, F32),
        ),
        in_specs=[hbm, hbm, smem, smem, hbm, hbm, hbm, hbm, hbm],
        out_specs=(hbm, hbm),
        scratch_shapes=[
            vmem((3, TEMB + TXT, WIN), BF16),
            vmem((3, ROWS, QUARTER), BF16),
            vmem((3, CH, D), BF16),
            vmem((3, CH, QUARTER), BF16),
            vmem((256, 128), F32),
            vmem((256, 128), F32),
            vmem((1, TXT), BF16),
            vmem((8, WIN), F32),
            vmem((2, 8, WIN), F32),
            vmem((4, HALF, 128), BF16),
            vmem((3, HALF, 128), BF16),
            vmem((HALF, 128), F32),
            vmem((48, 128), BF16),
            vmem((3, 48, 128), BF16),
            vmem((48, 128), BF16),
            vmem((3, 48, 128), BF16),
            vmem((4, 48, 128), BF16),
            vmem((DP, 8, WIN), F32),
            vmem((3, CH, 128), F32),
            vmem((3, 384, 128), BF16),
            vmem((128, 256), BF16),
            vmem((WIN, 384), BF16),
            vmem((16, 128), BF16),
            vmem((15, 16, 128), BF16),
            vmem((16, 16, 128), BF16),
            vmem((256, 128), F32),
            vmem((ROWS, 128), BF16),
            vmem((3 * WIN, CH), BF16),
            vmem((CH, WIN), F32),
            vmem((256, 256), BF16),
            pltpu.SemaphoreType.DMA((9,)),
            pltpu.SemaphoreType.DMA((2,)),
            pltpu.SemaphoreType.DMA((N_SEM,)),
            pltpu.SemaphoreType.DMA((N_SEM,)),
        ],
        compiler_params=pltpu.CompilerParams(collective_id=0, has_side_effects=True),
        name="distill",
    )(
        gen_noise, renoise, gen_step, renoise_step, text_pooled, embed, mod_weight, proj_weight,
        unembed,
    )
    return pl.pallas_call(
        finish,
        out_shape=(
            jax.ShapeDtypeStruct((ROWS, QUARTER), F32),
            jax.ShapeDtypeStruct(gen_noise.shape, F32),
        ),
        in_specs=[hbm, hbm, hbm],
        out_specs=(hbm, hbm),
        scratch_shapes=[
            vmem((ROWS, 128), BF16),
            vmem((CH, QUARTER), BF16),
            vmem((256, 128), F32),
            vmem((ROWS, QUARTER), F32),
            pltpu.SemaphoreType.DMA((3,)),
            pltpu.SemaphoreType.DMA((3,)),
        ],
        name="finish",
    )(term, unembed, score)


def solution(mesh):
    return jax.shard_map(
        body,
        mesh=mesh,
        in_specs=(
            P("dp", "fsdp", None),
            P("dp", "fsdp", None),
            P("dp"),
            P("dp"),
            P("dp", None),
            P(),
            P(None, None, "fsdp"),
            P(None, "fsdp", "mp"),
            P(None, None, "mp"),
        ),
        out_specs=(P("fsdp", "mp"), P("dp", "fsdp", None)),
        check_vma=False,
    )
```

```python
import functools
import math

import jax
import jax.numpy as jnp
from jax import lax
from jax.experimental import pallas as pl
from jax.experimental.pallas import tpu as pltpu
from jax.sharding import PartitionSpec as P

D = 3072
CH = 64
TEMB = 256
TXT = 768

GUIDANCE = 3.5
EPS_NORM = 1e-06
EPS_GAP = 1e-05
HIGH = lax.Precision.HIGHEST
MESH = pl.DeviceIdType.MESH
F32 = jnp.float32
BF16 = jnp.bfloat16

MP = 4
DP = 4
NX = 4
NY = 4
SEQ = 8192
TOKENS = 32768
WIN = 384
ROWS = 192
HALF = 96
QUARTER = 768

S_MOD = 0
S_FOLD = 2
S_DIRECT = 5
S_X = 8
S_Y = 11
S_MAPS = 14
S_GEN = 17
S_SUM = 20
S_COL = 35
N_SEM = 50


def split3(values):
    high = values.astype(BF16)
    rest = values - high.astype(F32)
    mid = rest.astype(BF16)
    low = (rest - mid.astype(F32)).astype(BF16)
    return high, mid, low


def split2(values):
    high = values.astype(BF16)
    return high, (values - high.astype(F32)).astype(BF16)


def dot(left, right):
    return jnp.dot(left, right, preferred_element_type=F32)


def dot_nt(left, right):
    return lax.dot_general(left, right, (((1,), (1,)), ((), ())), preferred_element_type=F32)


def pack_pair(block):
    half = block.shape[0] // 2
    return jnp.concatenate([block[:half, :CH], block[half:, :CH]], axis=1)


def rounded_map(packed, shift):
    return jnp.concatenate([packed.astype(BF16), *split2(shift)], axis=0)


def summed_map(own, received):
    total = own[...].astype(F32)
    for k in range(3):
        total = total + received[k].astype(F32)
    return rounded_map(total[:32], total[32:40] + total[40:48])


def lanes(shape):
    return lax.broadcasted_iota(jnp.int32, shape, len(shape) - 1)


def sublanes(shape):
    return lax.broadcasted_iota(jnp.int32, shape, len(shape) - 2)


def doubled(packed):
    left = lanes(packed.shape) < CH
    turned = pltpu.roll(packed, CH, 1)
    zero = jnp.zeros_like(packed)
    return jnp.concatenate(
        [
            jnp.where(left, packed, zero),
            jnp.where(left, turned, zero),
            jnp.where(left, zero, turned),
            jnp.where(left, zero, packed),
        ],
        axis=0,
    )


def kernel(
    gen_noise, renoise, gen_step, renoise_step, text, embed, mod_weight, proj, unembed,
    term_out, score_out,
    modw_v, proj_v, emb_v, une_v, noise_v, renoise_v, text_v,
    mod_send, mod_recv, fold_send, fold_recv, direct_v,
    x_send, x_recv, y_send, y_recv, maps_v, gen_v,
    mean_v, cov_v, scaled_v, left_v, sum_send, sum_recv, col_v,
    score_v, term_v, weight_v, centre_v, direct_w,
    load_sem, out_sem, send_sem, recv_sem,
):
    m = lax.axis_index("mp")
    f = lax.axis_index("fsdp")
    d = lax.axis_index("dp")
    y, x = lax.div(f, NX), lax.rem(f, NX)
    pair, side = lax.div(f, 2), lax.rem(f, 2)

    def load(src, dst, slot):
        copy = pltpu.make_async_copy(src, dst, load_sem.at[slot])
        copy.start()
        return copy

    ld_text = load(text, text_v, 0)
    ld_mod = [load(mod_weight.at[k], modw_v.at[k], 1 + k) for k in range(3)]
    ld_une = load(unembed, une_v, 4)
    ld_proj = load(proj, proj_v, 5)

    def plane(dy, dx):
        return {"fsdp": lax.rem(y + dy, NY) * NX + lax.rem(x + dx, NX)}

    def column(dd, dm):
        return {"dp": lax.rem(d + dd, DP), "mp": lax.rem(m + dm, MP)}

    def farthest_first(steps):
        return sorted(steps, key=lambda step: -sum(min(n, 4 - n) for n in step))

    plane_steps = farthest_first([(a, b) for a in range(NY) for b in range(NX) if a or b])
    column_steps = farthest_first([(a, b) for a in range(DP) for b in range(MP) if a or b])

    barrier = pltpu.get_barrier_semaphore()
    for step in plane_steps:
        pl.semaphore_signal(barrier, inc=1, device_id=plane(*step), device_id_type=MESH)
    for step in column_steps:
        pl.semaphore_signal(barrier, inc=1, device_id=column(*step), device_id_type=MESH)

    def remote(src, dst, slot, device, recv_slot=None):
        return pltpu.make_async_remote_copy(
            src_ref=src,
            dst_ref=dst,
            send_sem=send_sem.at[slot],
            recv_sem=recv_sem.at[slot if recv_slot is None else recv_slot],
            device_id=device,
            device_id_type=MESH,
        )

    t_gen = gen_step[0].astype(F32)
    t_new = renoise_step[0].astype(F32)
    level = t_new / 1000.0
    lane = lanes((8, 128)).astype(F32)
    row8 = sublanes((8, 128))
    frequency = jnp.exp(-math.log(10000.0) * lane / 128)
    angles = jnp.where(row8 == 0, t_gen, t_new) * frequency
    waves = jnp.concatenate([jnp.cos(angles), jnp.sin(angles)], axis=1)
    ld_text.wait()
    words = jnp.broadcast_to(text_v[...].astype(F32), (8, TXT))
    words = jnp.where(sublanes((8, TXT)) < 2, words, 0.0)
    joined = jnp.concatenate([waves, words], axis=1)
    joined = joined / (1.0 + jnp.exp(-joined))
    vectors = jnp.concatenate([joined, jnp.zeros_like(joined)], axis=0).astype(BF16)

    ld_mod[0].wait()
    ld_emb = load(embed, emb_v, 6)
    out0 = dot(vectors, modw_v[0])
    ld_mod[1].wait()
    out1 = dot(vectors, modw_v[1])
    ld_mod[2].wait()
    ld_noise = load(gen_noise.at[0], noise_v, 7)
    ld_renoise = load(renoise.at[0], renoise_v, 8)
    out2 = dot(vectors, modw_v[2])
    guided = out1[2:3] + GUIDANCE * (out1[1:2] - out1[2:3])
    rows = sublanes((8, WIN))
    mod_send[...] = jnp.where(
        rows == 0, out0[0:1], jnp.where(rows == 1, guided, jnp.where(rows == 2, out2[1:2], 0.0))
    )

    pl.semaphore_wait(barrier, len(plane_steps) + len(column_steps))

    kind = lax.div(f, 8)
    first = 2 * lax.rem(f, 8)

    def mod_copy(k):
        return remote(
            mod_send, mod_recv.at[kind], S_MOD + k, {"fsdp": first + k}, recv_slot=S_MOD + kind
        )

    for k in range(2):
        @pl.when(first + k != f)
        def _():
            mod_copy(k).start()

    @pl.when(f == 0)
    def _():
        mod_recv[0] = mod_send[...]

    @pl.when(f == NX * NY - 1)
    def _():
        mod_recv[1] = mod_send[...]

    ld_une.wait()
    ld_proj.wait()
    for k in range(3):
        fold_send[k] = pack_pair(dot_nt(proj_v[k], une_v[k])).astype(BF16)
    ld_emb.wait()
    for k in range(3):
        own = emb_v[k, :, pl.ds(pl.multiple_of(m * QUARTER, 128), QUARTER)]
        fold_send[3, 32 * k : 32 * k + 32, :] = pack_pair(dot_nt(own, une_v[k])).astype(BF16)
    fold_copies = []
    for r in range(1, MP):
        target = lax.rem(m + r, MP)
        copy = remote(fold_send.at[target], fold_recv.at[r - 1], S_FOLD + r - 1, {"mp": target})
        copy.start()
        fold_copies.append(copy)

    for k in range(3):
        mean_v[k] = jnp.broadcast_to(
            jnp.mean(emb_v[k].astype(F32), axis=1, keepdims=True), (CH, 128)
        )

    def covariance(k):
        centred = emb_v[k].astype(F32) - mean_v[k][:, :1]
        parts = jnp.concatenate(split3(centred), axis=0)
        gram = dot_nt(parts, parts)
        gram = gram[:CH] + gram[CH : 2 * CH] + gram[2 * CH :]
        gram = (gram[:, :CH] + gram[:, CH : 2 * CH] + gram[:, 2 * CH :]) * (1.0 / D)
        cov_v[k] = jnp.concatenate(split3(doubled(pack_pair(gram))), axis=0)

    covariance(0)

    for copy in fold_copies:
        copy.wait_recv()
    folded = fold_send[m].astype(F32)
    for r in range(MP - 1):
        folded = folded + fold_recv[r].astype(F32)

    def direct_copy(r):
        return remote(direct_v, direct_v, S_DIRECT + r, {"mp": r}, recv_slot=S_DIRECT)

    @pl.when(m == MP - 1)
    def _():
        direct_v[...] = folded
        for r in range(MP - 1):
            direct_copy(r).start()

    model = jnp.minimum(m, 2)
    window = pl.ds(pl.multiple_of(pair * WIN, 128), WIN)
    centre_v[...] = emb_v[model, :, window].astype(F32) - mean_v[model][:, :1]
    weight = jnp.concatenate([folded[:, :CH], folded[:, CH:]], axis=0)
    none = jnp.zeros_like(weight)
    weight = jnp.concatenate(
        [jnp.where(side == 0, weight, none), jnp.where(side == 0, none, weight)], axis=0
    )
    high, low = split2(weight)
    weight_v[...] = jnp.concatenate([high, low, high], axis=0)

    @pl.when(f != 0)
    def _():
        remote(mod_send, mod_recv.at[0], S_MOD, {"fsdp": first}).wait_recv()

    @pl.when(f != NX * NY - 1)
    def _():
        remote(mod_send, mod_recv.at[1], S_MOD + 1, {"fsdp": first}).wait_recv()

    shift = mod_recv[0, pl.ds(m, 1), :]
    gain = 1.0 + mod_recv[1, pl.ds(m, 1), :]
    left = jnp.concatenate([centre_v[...] * gain, jnp.broadcast_to(shift, (8, WIN))], axis=0)
    high, low = split2(left)
    result = dot(jnp.concatenate([high, high, low], axis=1), weight_v[...])
    x_send[...] = rounded_map(
        pack_pair(result[:CH]), jnp.concatenate([result[CH:], result[CH:]], axis=1)
    )

    x_copies = []
    for r in range(1, NX):
        copy = remote(x_send, x_recv.at[r - 1], S_X + r - 1, plane(0, r))
        copy.start()
        x_copies.append(copy)

    gen_v[d] = jnp.where(
        rows == 0, mod_recv[0, 0:1, :], jnp.where(rows == 1, mod_recv[1, 0:1, :], 0.0)
    )
    gen_copies = []
    for r in range(1, DP):
        copy = remote(gen_v.at[d], gen_v.at[d], S_GEN + r - 1, {"dp": lax.rem(d + r, DP)})
        copy.start()
        gen_copies.append(copy)

    covariance(1)
    for copy in x_copies:
        copy.wait_recv()
    y_send[...] = summed_map(x_send, x_recv)
    y_copies = []
    for r in range(1, NY):
        copy = remote(y_send, y_recv.at[r - 1], S_Y + r - 1, plane(r, 0))
        copy.start()
        y_copies.append(copy)
    covariance(2)
    for copy in y_copies:
        copy.wait_recv()
    maps_v[m] = summed_map(y_send, y_recv)
    map_copies = []
    for r in range(1, MP):
        copy = remote(maps_v.at[m], maps_v.at[m], S_MAPS + r - 1, {"mp": lax.rem(m + r, MP)})
        copy.start()
        map_copies.append(copy)

    ones = jnp.where(
        (lanes((128, 128)) < CH) == (sublanes((128, 128)) < CH), 1.0, 0.0
    ).astype(BF16)
    ones = jnp.concatenate([ones, ones, ones], axis=0)

    def inverse_std(values, k):
        thrice = jnp.concatenate([values, values, values], axis=1)
        energy = dot(thrice, cov_v[k]) * values.astype(F32)
        energy = jnp.concatenate(split3(energy), axis=1)
        return lax.rsqrt(jnp.maximum(dot(energy, ones), 0.0) + EPS_NORM)

    def stacked(packed):
        return jnp.concatenate(split2(doubled(packed)), axis=0)

    ld_noise.wait()
    latent = noise_v[...].astype(BF16)
    gen_scale = inverse_std(latent, 0)
    scaled_v[...] = jnp.transpose(latent.astype(F32) * gen_scale).astype(BF16)
    twice = jnp.concatenate([latent, latent], axis=1)

    @pl.when(m != MP - 1)
    def _():
        remote(direct_v, direct_v, S_DIRECT, {"mp": MP - 1}).wait_recv()

    gen_direct = dot(twice, stacked(direct_v[0:32, :]))
    direct_w[:, :128] = stacked(direct_v[32:64, :])
    direct_w[:, 128:] = stacked(direct_v[64:96, :])
    ld_renoise.wait()

    for copy in map_copies:
        copy.wait_recv()

    def map_of(k):
        return doubled(maps_v[k, 0:32, :].astype(F32)).astype(BF16)

    def shift_of(k):
        rows16 = maps_v[k, 32:48, :].astype(F32)
        return rows16[0:1] + rows16[8:9]

    clean = gen_direct + gen_scale * dot(latent, map_of(0)) + shift_of(0)
    noisy = (1.0 - level) * clean + level * renoise_v[...]
    values = noisy.astype(BF16)
    twice = jnp.concatenate([values, values], axis=1)
    direct = dot(twice, direct_w[...])
    mapped = dot(values, jnp.concatenate([map_of(1), map_of(2)], axis=1))
    real = direct[:, :128] + inverse_std(values, 1) * mapped[:, :128] + shift_of(1)
    fake = direct[:, 128:] + inverse_std(values, 2) * mapped[:, 128:] + shift_of(2)
    gap = level * (real - fake)
    distance = jnp.abs(clean - noisy + level * real)

    moment = dot(scaled_v[...], gap.astype(BF16))
    moment = moment[:CH] + pltpu.roll(moment[CH:], CH, 1)
    left32 = lanes((32, 128)) < CH
    moment = jnp.where(left32, moment[:32], pltpu.roll(moment[32:], CH, 1))
    piece = moment[0:8]
    for k in range(1, MP):
        piece = jnp.where(m == k, moment[8 * k : 8 * k + 8], piece)
    total = jnp.sum(gap, axis=0, keepdims=True)
    total = total + pltpu.roll(total, CH, 1)
    spread = jnp.sum(distance, axis=0, keepdims=True)
    tail = []
    for term in split2(total) + split2(spread):
        tail.append(jnp.broadcast_to(term.astype(F32), (8, 128)))
    tail = jnp.where(
        row8 == 0, tail[0], jnp.where(row8 == 1, tail[1], jnp.where(row8 == 2, tail[2], tail[3]))
    )
    tail = jnp.where(row8 < 4, tail, 0.0)
    sum_send[...] = jnp.concatenate([piece, tail], axis=0).astype(BF16)
    sum_copies = []
    for k, step in enumerate(plane_steps):
        copy = remote(sum_send, sum_recv.at[k], S_SUM + k, plane(*step))
        copy.start()
        sum_copies.append(copy)

    for copy in gen_copies:
        copy.wait_recv()
    centred = emb_v[0, :, window].astype(F32) - mean_v[0][:, :1]
    pieces = [centred[:32] * (1.0 + gen_v[s, 1:2, :]) for s in range(DP)]
    pieces += [centred[32:] * (1.0 + gen_v[s, 1:2, :]) for s in range(DP)]
    pieces += [jnp.where(rows == 0, gen_v[s], 0.0) for s in range(DP)]
    pieces += [jnp.zeros((96, WIN), F32)]
    left_v[...] = jnp.transpose(jnp.concatenate(pieces, axis=0)).astype(BF16)

    for copy in sum_copies:
        copy.wait_recv()
    sums = sum_send[...].astype(F32)
    for k in range(len(plane_steps)):
        sums = sums + sum_recv[k].astype(F32)
    spread = sums[10:11, :] + sums[11:12, :]
    gap_scale = jnp.sum(spread, axis=1, keepdims=True) / (SEQ * CH) + EPS_GAP
    total = jnp.where(row8 == 0, sums[8:9, :] + sums[9:10, :], 0.0)
    sums = jnp.concatenate([sums[0:8], total], axis=0)
    slot = d * MP + m
    col_v[slot] = (sums / (gap_scale * math.sqrt(TOKENS))).astype(BF16)
    col_copies = []
    for k, step in enumerate(column_steps):
        copy = remote(col_v.at[slot], col_v.at[slot], S_COL + k, column(*step))
        copy.start()
        col_copies.append(copy)
    score_v[...] = gap / gap_scale
    score_copy = pltpu.make_async_copy(score_v, score_out.at[0], out_sem.at[0])
    score_copy.start()

    for k in range(2):
        @pl.when(first + k != f)
        def _():
            mod_copy(k).wait_send()

    @pl.when(m == MP - 1)
    def _():
        for r in range(MP - 1):
            direct_copy(r).wait_send()

    for copy in fold_copies + x_copies + y_copies + map_copies + gen_copies + sum_copies:
        copy.wait_send()
    score_copy.wait()

    for copy in col_copies:
        copy.wait_recv()
    table = [col_v[k].astype(F32) for k in range(DP * MP)]
    block = jnp.concatenate([entry[:8] for entry in table], axis=0)
    right = jnp.concatenate(
        [block, pltpu.roll(block, CH, 1)]
        + [table[MP * s][8:] for s in range(DP)]
        + [jnp.zeros((96, 128), F32)],
        axis=0,
    ).astype(BF16)
    own_rows = left_v[pl.ds(pl.multiple_of(side * ROWS, 64), ROWS), :]
    term_v[...] = dot(own_rows, right).astype(BF16)
    term_copy = pltpu.make_async_copy(term_v, term_out, out_sem.at[1])
    term_copy.start()

    for copy in col_copies:
        copy.wait_send()
    term_copy.wait()


def finish(
    term, unembed, score, grad_out, score_out, term_v, une_v, score_v, grad_v, in_sem, out_sem
):
    loads = [
        pltpu.make_async_copy(src, dst, in_sem.at[k])
        for k, (src, dst) in enumerate(
            [(term, term_v), (unembed.at[0], une_v), (score.at[0], score_v)]
        )
    ]
    for copy in loads:
        copy.start()
    loads[0].wait()
    loads[1].wait()
    stores = []
    for k in range(2):
        rows = slice(HALF * k, HALF * k + HALF)
        grad_v[rows, :] = dot(term_v[rows, :CH], une_v[...])
        copy = pltpu.make_async_copy(grad_v.at[rows], grad_out.at[rows], out_sem.at[k])
        copy.start()
        stores.append(copy)
    loads[2].wait()
    copy = pltpu.make_async_copy(score_v, score_out.at[0], out_sem.at[2])
    copy.start()
    stores.append(copy)
    for copy in stores:
        copy.wait()


def body(
    gen_noise, renoise, gen_step, renoise_step, text_pooled, embed, mod_weight, proj_weight, unembed
):
    hbm = pl.BlockSpec(memory_space=pl.ANY)
    smem = pl.BlockSpec(memory_space=pltpu.SMEM)
    vmem = pltpu.VMEM
    term, score = pl.pallas_call(
        kernel,
        out_shape=(
            jax.ShapeDtypeStruct((ROWS, 128), BF16),
            jax.ShapeDtypeStruct(gen_noise.shape, F32),
        ),
        in_specs=[hbm, hbm, smem, smem, hbm, hbm, hbm, hbm, hbm],
        out_specs=(hbm, hbm),
        scratch_shapes=[
            vmem((3, TEMB + TXT, WIN), BF16),
            vmem((3, ROWS, QUARTER), BF16),
            vmem((3, CH, D), BF16),
            vmem((3, CH, QUARTER), BF16),
            vmem((256, 128), F32),
            vmem((256, 128), F32),
            vmem((1, TXT), BF16),
            vmem((8, WIN), F32),
            vmem((2, 8, WIN), F32),
            vmem((4, HALF, 128), BF16),
            vmem((3, HALF, 128), BF16),
            vmem((HALF, 128), F32),
            vmem((48, 128), BF16),
            vmem((3, 48, 128), BF16),
            vmem((48, 128), BF16),
            vmem((3, 48, 128), BF16),
            vmem((4, 48, 128), BF16),
            vmem((DP, 8, WIN), F32),
            vmem((3, CH, 128), F32),
            vmem((3, 384, 128), BF16),
            vmem((128, 256), BF16),
            vmem((WIN, 384), BF16),
            vmem((16, 128), BF16),
            vmem((15, 16, 128), BF16),
            vmem((16, 16, 128), BF16),
            vmem((256, 128), F32),
            vmem((ROWS, 128), BF16),
            vmem((3 * WIN, CH), BF16),
            vmem((CH, WIN), F32),
            vmem((256, 256), BF16),
            pltpu.SemaphoreType.DMA((9,)),
            pltpu.SemaphoreType.DMA((2,)),
            pltpu.SemaphoreType.DMA((N_SEM,)),
            pltpu.SemaphoreType.DMA((N_SEM,)),
        ],
        compiler_params=pltpu.CompilerParams(collective_id=0, has_side_effects=True),
        name="distill",
    )(
        gen_noise, renoise, gen_step, renoise_step, text_pooled, embed, mod_weight, proj_weight,
        unembed,
    )
    return pl.pallas_call(
        finish,
        out_shape=(
            jax.ShapeDtypeStruct((ROWS, QUARTER), F32),
            jax.ShapeDtypeStruct(gen_noise.shape, F32),
        ),
        in_specs=[hbm, hbm, hbm],
        out_specs=(hbm, hbm),
        scratch_shapes=[
            vmem((ROWS, 128), BF16),
            vmem((CH, QUARTER), BF16),
            vmem((256, 128), F32),
            vmem((ROWS, QUARTER), F32),
            pltpu.SemaphoreType.DMA((3,)),
            pltpu.SemaphoreType.DMA((3,)),
        ],
        name="finish",
    )(term, unembed, score)


def solution(mesh):
    return jax.shard_map(
        body,
        mesh=mesh,
        in_specs=(
            P("dp", "fsdp", None),
            P("dp", "fsdp", None),
            P("dp"),
            P("dp"),
            P("dp", None),
            P(),
            P(None, None, "fsdp"),
            P(None, "fsdp", "mp"),
            P(None, None, "mp"),
        ),
        out_specs=(P("fsdp", "mp"), P("dp", "fsdp", None)),
        check_vma=False,
    )
```
